32 devices in a mesh: fsdp: 2 (over y), ctx: 4 (over z), tp: 4 (over x, core).
Axes of the slice: x: 2, y: 2, z: 4, core: 2. Of those that a mesh axis runs over, the one named last changes fastest.
Arguments:
- layer_input: bfloat16 [4, 2048, 2048], P('fsdp', 'ctx'), may hold values from -6 to 6
- segment_ids: int32 [4, 2048], P('fsdp', 'ctx'), may hold values from 0 to 15, never falling along the last dimension, each value on 1 to 1536 neighbouring positions
- qkv_weight: bfloat16 [2048, 3, 2048], P('fsdp', None, 'tp'), may hold values from -0.125 to 0.125
- qv_bias: bfloat16 [2, 2048], P(None, 'tp'), may hold values from -1.1953125 to 1.1953125
- out_weight: bfloat16 [2048, 2048], P('tp', 'fsdp'), may hold values from -1.5 to 1.5
- out_bias: bfloat16 [2048], replicated, may hold values from -1.1953125 to 1.1953125
- norm1_gain: bfloat16 [2048], replicated, may hold values from 0.5 to 1.5
- norm1_bias: bfloat16 [2048], replicated, may hold values from -1.1953125 to 1.1953125
- up_weight: bfloat16 [2048, 8192], P('fsdp', 'tp'), may hold values from -0.125 to 0.125
- up_bias: bfloat16 [8192], P('tp'), may hold values from -1.1953125 to 1.1953125
- down_weight: bfloat16 [8192, 2048], P('tp', 'fsdp'), may hold values from -0.0625 to 0.0625
- down_bias: bfloat16 [2048], replicated, may hold values from -1.1953125 to 1.1953125
- norm2_gain: bfloat16 [2048], replicated, may hold values from 0.5 to 1.5
- norm2_bias: bfloat16 [2048], replicated, may hold values from -1.1953125 to 1.1953125
- out_grad: bfloat16 [4, 2048, 2048], P('fsdp', 'ctx'), may hold values from -6 to 6
Outputs:
- layer_output: bfloat16 [4, 2048, 2048], P('fsdp', 'ctx')
- input_grad: float32 [4, 2048, 2048], P('fsdp', 'ctx')
- qkv_weight_grad: float32 [2048, 3, 2048], P('fsdp', None, 'tp')
- qv_bias_grad: float32 [2, 2048], P(None, 'tp')
- out_weight_grad: float32 [2048, 2048], P('tp', 'fsdp')
- out_bias_grad: float32 [2048], replicated
- norm1_gain_grad: float32 [2048], replicated
- norm1_bias_grad: float32 [2048], replicated
- up_weight_grad: float32 [2048, 8192], P('fsdp', 'tp')
- up_bias_grad: float32 [8192], P('tp')
- down_weight_grad: float32 [8192, 2048], P('tp', 'fsdp')
- down_bias_grad: float32 [2048], replicated
- norm2_gain_grad: float32 [2048], replicated
- norm2_bias_grad: float32 [2048], replicated
The draws below stay inside these ranges and needn't reach their ends.
Inputs may be any that keep to these rules, and one draw needn't show every extreme that they name: `segment_ids`: along each row the ids never fall, and each id names 1 to 1536 tokens in a row; in every row one id names exactly 1536 tokens.
All inputs are finite; a program needn't handle non-finite values.
Results may differ from the reference program's by a relative error of at most 0.013.
Values may be sent and summed in bfloat16 or wider, within the bound.
No kernel may reach another device: no remote copies, remote signals or barrier semaphores. Data moves between devices by JAX's collectives and lax.ppermute only.
A program may use at most 320 MiB of HBM per device.

```python
import math
import jax
import jax.numpy as jnp
import numpy as np
from jax import lax

D = 2048
HEADS = 16
HEAD = 128
FF = 8192
LEN = 2048
SEGS = 16
ROWS = 4


def with_spikes(entries, key, source, target, parts, factor):
    def block_of(position):
        return (jnp.arange(entries.shape[position]) // (entries.shape[position] // parts)).reshape((-1,) + (1,) * (entries.ndim - 1 - position))

    near = jax.random.permutation(key, parts)[block_of(target)]
    second = (block_of(target) + parts // 2) % parts
    return jnp.where((block_of(source) == near) | (block_of(source) == second), factor * entries, entries)


def levels(key, shape, pieces, smallest, top_value):
    level = 1.0
    for axis_at, shards_of in pieces:
        steps = jax.random.uniform(jax.random.fold_in(jax.random.fold_in(key, 6), axis_at), (shards_of,), jnp.float32, smallest / len(pieces), top_value / len(pieces))
        level = level * jnp.repeat(jnp.exp(steps), shape[axis_at] // shards_of).reshape((-1,) + (1,) * (len(shape) - 1 - axis_at))
    return level


def length_profile(amount, total, limit, skew):
    weights = [(1 << 20) // math.isqrt(standing ** skew) + 1 for standing in range(2, amount + 1)]
    rest, holding = total - limit - (amount - 1), [1] * (amount - 1)
    while rest > 0:
        movable = [i for i in range(amount - 1) if holding[i] < limit]
        mass, left = sum([weights[i] for i in movable]), rest
        for i in movable:
            extra = min(limit - holding[i], max(1, left * weights[i] // mass), rest)
            holding[i] = holding[i] + extra
            rest = rest - extra
    return np.array([limit] + holding)


def uneven_parts(key, count, total, limit, skew):
    if count == 2:
        one = jax.random.randint(key, (), max(1, total - limit), min(limit, total - 1) + 1)
        return jnp.stack([one, total - one])
    tallies = jnp.asarray(length_profile(count, total, limit, skew), jnp.int32)
    pairs = (count - 1) // 2
    donor, receiver = tallies[1:1 + 2 * pairs:2], tallies[2:2 + 2 * pairs:2]
    room = jnp.minimum(donor - 1, limit - receiver)
    moved = jax.random.randint(jax.random.fold_in(key, 1), (pairs,), 0, 1 << 20) % (room + 1)
    tallies = tallies.at[1:1 + 2 * pairs:2].set(donor - moved).at[2:2 + 2 * pairs:2].set(receiver + moved)
    return tallies[jax.random.permutation(jax.random.fold_in(key, 2), count)]


def centred(key, shape, scale, reach, split=(), held_as=jnp.bfloat16):
    values = jax.random.normal(key, shape, jnp.float32) * scale
    if len(split) > 0:
        values = levels(key, shape, split, -0.22, 0.18) * values
    return jnp.clip(values, min=-reach, max=reach).astype(held_as)


def noise_with(own_key, dims, scale, reach, pieces, heavy, held_as=jnp.bfloat16):
    entries = scale * jax.random.normal(own_key, dims, jnp.float32)
    if pieces:
        entries = entries * levels(own_key, dims, pieces, -0.22, 0.18)
    return jnp.clip(with_spikes(entries, jax.random.fold_in(own_key, 3), *heavy), -reach, reach).astype(held_as)


def setup_inputs(seed: int = 0) -> dict:
    splits = jax.random.split(jax.random.key(seed), 16)
    return {
        "layer_input": centred(splits[0], (ROWS, LEN, D), 1.0, 6.0, ((0, 2), (1, 4))),
        "segment_ids": jax.vmap(lambda own: jnp.searchsorted(jnp.cumsum(uneven_parts(own, SEGS, LEN, 3 * LEN // 4, 2)), jnp.arange(LEN), side="right"))(jax.random.split(splits[1], ROWS)).reshape((ROWS, LEN)).astype(jnp.int32),
        "qkv_weight": centred(splits[2], (D, 3, D), D ** -0.5, 0.125, ((0, 2), (2, 4))),
        "qv_bias": centred(splits[3], (2, D), 0.2, 1.1953125, ((1, 4),)),
        "out_weight": centred(splits[4], (D, D), (max(D // 128, 1)) ** -0.5, 1.5, ((0, 4), (1, 2))),
        "out_bias": centred(splits[5], (D,), 0.2, 1.1953125),
        "norm1_gain": jnp.clip(1.0 + 0.1 * jax.random.normal(splits[6], (D,), jnp.float32), 0.5, 1.5).astype(jnp.bfloat16),
        "norm1_bias": centred(splits[7], (D,), 0.2, 1.1953125),
        "up_weight": centred(splits[8], (D, FF), D ** -0.5, 0.125, ((0, 2), (1, 4))),
        "up_bias": centred(splits[9], (FF,), 0.2, 1.1953125, ((0, 4),)),
        "down_weight": centred(splits[10], (FF, D), FF ** -0.5, 0.0625, ((0, 4), (1, 2))),
        "down_bias": centred(splits[11], (D,), 0.2, 1.1953125),
        "norm2_gain": jnp.clip(1.0 + 0.1 * jax.random.normal(splits[12], (D,), jnp.float32), 0.5, 1.5).astype(jnp.bfloat16),
        "norm2_bias": centred(splits[13], (D,), 0.2, 1.1953125),
        "out_grad": noise_with(splits[14], (ROWS, LEN, D), 1.0, 6.0, ((0, 2), (1, 4)), (0, 2, 2, 2.0)),
    }


PRECISE = lax.Precision.HIGHEST
EPSILON = 1e-12
NEGATIVE = -1e+30

@jax.custom_vjp
def low(v):
    return lax.optimization_barrier(v.astype(jnp.bfloat16)).astype(jnp.float32)

@jax.custom_vjp
def low_back(v):
    return v

def low_keep(v):
    return (low(v), None)

def low_pass(kept, grad):
    return (grad,)

def back_keep(v):
    return (v, None)

def back_low(kept, grad):
    return (low(grad),)
low.defvjp(low_keep, low_pass)
low_back.defvjp(back_keep, back_low)

def layer_norm(hidden, gain, shift):
    center = hidden - lax.optimization_barrier(jnp.mean(hidden, axis=-1, keepdims=True))
    spread = lax.optimization_barrier(jnp.mean(center * center, axis=-1, keepdims=True))
    return center * lax.rsqrt(spread + EPSILON) * gain + shift

def gelu_tanh(pre):
    return 0.5 * pre * (1.0 + jnp.tanh(0.7978845608028654 * (pre + 0.044715 * pre * pre * pre)))

def attend(queries, keys, values, segments):
    length = queries.shape[0]
    query_heads = queries.reshape(length, HEADS, HEAD)
    key_heads = keys.reshape(length, HEADS, HEAD)
    value_heads = values.reshape(length, HEADS, HEAD)
    raw = low_back(jnp.einsum('qhd,khd->hqk', query_heads, key_heads, precision=PRECISE) * (1.0 / math.sqrt(HEAD)))
    same = segments[:, None] == segments[None, :]
    scores = jnp.where(same[None], raw, NEGATIVE)
    top = lax.optimization_barrier(jnp.max(scores, axis=-1, keepdims=True))
    log_total = top + jnp.log(lax.optimization_barrier(jnp.sum(jnp.exp(scores - top), axis=-1, keepdims=True)))
    probs = low(jnp.exp(scores - log_total))
    return jnp.einsum('hqk,khd->qhd', probs, value_heads, precision=PRECISE).reshape(length, D)

def layer_row(hidden, segments, joint_weight, bias_pair, output_weight, output_bias, gain_one, shift_one, upward_weight, upward_bias, downward_weight, downward_bias, gain_two, shift_two):
    projections = jnp.einsum('ld,dce->lce', hidden, joint_weight, precision=PRECISE)
    queries = low(low_back(projections[:, 0] + bias_pair[0]))
    keys = low(low_back(projections[:, 1]))
    values = low(low_back(projections[:, 2] + bias_pair[1]))
    attended = low(low_back(jax.checkpoint(attend)(queries, keys, values, segments)))
    attn_out = low_back(jnp.dot(attended, output_weight, precision=PRECISE) + output_bias)
    norm_one = layer_norm(hidden + attn_out, gain_one, shift_one)
    pre_act = low_back(jnp.dot(low(norm_one), upward_weight, precision=PRECISE) + upward_bias)
    act_low = low(gelu_tanh(pre_act))
    mlp_out = low_back(jnp.dot(act_low, downward_weight, precision=PRECISE) + downward_bias)
    return layer_norm(norm_one + mlp_out, gain_two, shift_two)

def reference(layer_input, segment_ids, qkv_weight, qv_bias, out_weight, out_bias, norm1_gain, norm1_bias, up_weight, up_bias, down_weight, down_bias, norm2_gain, norm2_bias, out_grad):
    params = tuple((weight.astype(jnp.float32) for weight in (qkv_weight, qv_bias, out_weight, out_bias, norm1_gain, norm1_bias, up_weight, up_bias, down_weight, down_bias, norm2_gain, norm2_bias)))
    starting = tuple((jnp.zeros_like(weight) for weight in params))

    def one_row(totals, row_data):
        row_input, row_segments, row_grad = row_data

        def forward(hidden, *weights):
            return layer_row(hidden, row_segments, *weights)
        result, pullback = jax.vjp(forward, row_input.astype(jnp.float32), *params)
        grads = pullback(row_grad.astype(jnp.float32))
        totals = tuple((total + grad for total, grad in zip(totals, grads[1:])))
        return (totals, (result.astype(jnp.bfloat16), grads[0]))
    totals, (outputs, input_grads) = lax.scan(one_row, starting, (layer_input, segment_ids, out_grad))
    return (outputs, input_grads, totals[0], totals[1], totals[2], totals[3], totals[4], totals[5], totals[6], totals[7], totals[8], totals[9], totals[10], totals[11])
```

```python
import functools
import math

import jax
import jax.numpy as jnp
from jax import lax
from jax.experimental import pallas as pl
from jax.experimental.pallas import tpu as pltpu
from jax.sharding import PartitionSpec as P

HEAD = 128
EPSILON = 1e-12
NEGATIVE = -1e30
LOG2E = 1.4426950408889634
VMEM_LIMIT = 56 * 2**20

BF16 = jnp.bfloat16
F32 = jnp.float32


def dot(left, right, left_dim, right_dim):
    return lax.dot_general(
        left, right, (((left_dim,), (right_dim,)), ((), ())), preferred_element_type=F32
    )


def core_swap(value):
    size = lax.axis_size("tp")
    return lax.ppermute(value, "tp", [(i, i ^ 1) for i in range(size)])


def chip_swap(value):
    size = lax.axis_size("tp")
    return lax.ppermute(value, "tp", [(i, i ^ 2) for i in range(size)])


def shift(value, axis, by):
    size = lax.axis_size(axis)
    return lax.ppermute(value, axis, [(i, (i + by) % size) for i in range(size)])


def after(value, *others):
    return lax.optimization_barrier((value, *others))[0]


def line_sum(value):
    first = lax.ppermute(value, "ctx", [(0, 1), (3, 2)])
    pair = (value.astype(F32) + first.astype(F32)).astype(BF16)
    second = lax.ppermute(pair, "ctx", [(1, 2), (2, 1)])
    total = (pair.astype(F32) + second.astype(F32)).astype(BF16)
    third = lax.ppermute(total, "ctx", [(1, 0), (2, 3)])
    place = lax.axis_index("ctx")
    return jnp.where((place == 0) | (place == 3), third, total)


def rotate(value, axis, by, count):
    size = value.shape[axis]
    block = size // count
    if count == 1:
        return value
    twice = jnp.concatenate([value, value], axis=axis)
    if count == 2:
        swapped = lax.slice_in_dim(twice, block, block + size, axis=axis)
        return jnp.where(by == 0, value, swapped)
    return lax.dynamic_slice_in_dim(twice, by * block, size, axis=axis)


def project_kernel(blocks, x_ref, *refs):
    weights, bias_ref, outs = refs[:blocks], refs[blocks], refs[blocks + 1 :]
    total = bias_ref[...].astype(F32)
    depth = x_ref.shape[1] // blocks
    acc = None
    for index, weight in enumerate(weights):
        part = dot(x_ref[:, index * depth : (index + 1) * depth], weight[...], 1, 0)
        acc = part if acc is None else acc + part
    low = (acc + total).astype(BF16)
    for slot, out in enumerate(outs):
        out[...] = low[:, slot * HEAD : (slot + 1) * HEAD]


def project(x, weights, bias):
    tokens, width = x.shape
    columns = weights[0].shape[1]
    heads = columns // HEAD
    tile = 512
    return pl.pallas_call(
        functools.partial(project_kernel, len(weights)),
        grid=(tokens // tile,),
        in_specs=[pl.BlockSpec((tile, width), lambda i: (i, 0))]
        + [pl.BlockSpec(w.shape, lambda i: (0, 0)) for w in weights]
        + [pl.BlockSpec((1, columns), lambda i: (0, 0))],
        out_specs=[pl.BlockSpec((tile, HEAD), lambda i: (i, 0))] * heads,
        out_shape=[jax.ShapeDtypeStruct((tokens, HEAD), BF16)] * heads,
        compiler_params=pltpu.CompilerParams(vmem_limit_bytes=VMEM_LIMIT),
        cost_estimate=pl.CostEstimate(
            flops=2 * tokens * width * columns,
            bytes_accessed=2 * (tokens * width + width * columns + tokens * columns),
            transcendentals=0,
        ),
        name="project",
    )(x, *weights, bias)


def grad_kernel(pairs, has_add, *refs):
    out = refs[-1]
    acc = None
    for index in range(pairs):
        part = dot(refs[2 * index][...], refs[2 * index + 1][...], 0, 0)
        acc = part if acc is None else acc + part
    if has_add:
        acc = acc + refs[2 * pairs][...].astype(F32)
    out[...] = acc.astype(out.dtype)


def weight_grad(lefts, rights, left_cols, right_cols, add=None):
    row_from, rows = left_cols
    col_from, cols = right_cols
    row_tile, col_tile = min(1024, rows), min(512, cols)
    depth = sum(v.shape[0] for v in lefts)
    specs, values = [], []
    row_base, col_base = row_from // row_tile, col_from // col_tile
    for left, right in zip(lefts, rights):
        specs.append(pl.BlockSpec((left.shape[0], row_tile), lambda i, j: (0, i + row_base)))
        specs.append(pl.BlockSpec((right.shape[0], col_tile), lambda i, j: (0, j + col_base)))
        values += [left, right]
    if add is not None:
        specs.append(pl.BlockSpec((row_tile, col_tile), lambda i, j: (i, j)))
        values.append(add)
    return pl.pallas_call(
        functools.partial(grad_kernel, len(lefts), add is not None),
        grid=(rows // row_tile, cols // col_tile),
        in_specs=specs,
        out_specs=pl.BlockSpec((row_tile, col_tile), lambda i, j: (i, j)),
        out_shape=jax.ShapeDtypeStruct((rows, cols), BF16),
        compiler_params=pltpu.CompilerParams(vmem_limit_bytes=VMEM_LIMIT),
        cost_estimate=pl.CostEstimate(
            flops=2 * rows * cols * depth,
            bytes_accessed=2 * (depth * rows + depth * cols + 2 * rows * cols),
            transcendentals=0,
        ),
        name="weight_grad",
    )(*values)


def gather_blocks(scratch, sources):
    size = sources[0].shape[0]
    for index, source in enumerate(sources):
        scratch[index * size : (index + 1) * size, :] = source[...]


def attend_kernel(parts, block, live, *refs):
    q_in, k_in, v_in = refs[:parts], refs[parts : 2 * parts], refs[2 * parts : 3 * parts]
    seg_row, seg_col = refs[3 * parts : 3 * parts + 2]
    outs = refs[3 * parts + 2 : 4 * parts + 2]
    mixed_ref, total_ref = refs[4 * parts + 2 : 4 * parts + 4]
    qs, ks, vs, scores, top, total, mixed = refs[4 * parts + 4 :]
    at = pl.program_id(0)
    count = qs.shape[0] // block

    @pl.when(at == 0)
    def _():
        gather_blocks(qs, q_in)
        gather_blocks(ks, k_in)
        gather_blocks(vs, v_in)

    here = pl.multiple_of(at * block, block)
    query = qs[pl.ds(here, block), :]
    seg_query = seg_row[:, pl.ds(here, block)]
    top[...] = jnp.full_like(top, NEGATIVE)
    total[...] = jnp.zeros_like(total)
    mixed[...] = jnp.zeros_like(mixed)

    def score(step, masked):
        rows = pl.ds(pl.multiple_of(step * block, block), block)
        raw = dot(ks[rows, :], query, 1, 1) * (LOG2E / math.sqrt(HEAD))
        if masked:
            raw = jnp.where(seg_col[rows, 0:1] == seg_query, raw, NEGATIVE)
        scores[rows, :] = raw
        top[...] = jnp.maximum(top[...], jnp.max(raw, axis=0, keepdims=True))

    def first(step, carry):
        pl.when(live[at, step] == 1)(functools.partial(score, step, True))
        pl.when(live[at, step] == 2)(functools.partial(score, step, False))
        return carry

    def second(step, carry):
        @pl.when(live[at, step] > 0)
        def _():
            rows = pl.ds(pl.multiple_of(step * block, block), block)
            weight = jnp.exp2(scores[rows, :] - top[...])
            total[...] += jnp.sum(weight, axis=0, keepdims=True)
            mixed[...] += dot(vs[rows, :], weight.astype(BF16), 0, 0)

        return carry

    lax.fori_loop(0, count, first, 0)
    lax.fori_loop(0, count, second, 0)
    result = mixed[...] / total[...]
    mixed_ref[:, pl.ds(here, block)] = result
    total_ref[:, pl.ds(here, block)] = top[...] + jnp.log2(total[...])
    low = result.T.astype(BF16)
    per = count // parts
    for slot, out in enumerate(outs):

        @pl.when(at // per == slot)
        def _(out=out):
            out[pl.ds(pl.multiple_of((at % per) * block, block), block), :] = low


def attend(row, queries, keys, values, seg_row, seg_col, live):
    parts = len(queries)
    length = seg_row.shape[2]
    size = length // parts
    block = length // live.shape[1]
    part_spec = pl.BlockSpec((size, HEAD), lambda i, s: (row, 0))
    whole = lambda i, s: (0, 0)
    flops = 2 * 2 * length * length * HEAD * 5 // 8
    return pl.pallas_call(
        functools.partial(attend_kernel, parts, block),
        grid_spec=pltpu.PrefetchScalarGridSpec(
            num_scalar_prefetch=1,
            grid=(length // block,),
            in_specs=[part_spec] * (3 * parts)
            + [
                pl.BlockSpec((None, 1, length), lambda i, s: (row, 0, 0)),
                pl.BlockSpec((None, length, HEAD), lambda i, s: (row, 0, 0)),
            ],
            out_specs=[pl.BlockSpec((size, HEAD), whole)] * parts
            + [pl.BlockSpec((HEAD, length), whole), pl.BlockSpec((1, length), whole)],
            scratch_shapes=[pltpu.VMEM((length, HEAD), BF16)] * 3
            + [
                pltpu.VMEM((length, block), F32),
                pltpu.VMEM((1, block), F32),
                pltpu.VMEM((1, block), F32),
                pltpu.VMEM((HEAD, block), F32),
            ],
        ),
        out_shape=[jax.ShapeDtypeStruct((size, HEAD), BF16)] * parts
        + [
            jax.ShapeDtypeStruct((HEAD, length), F32),
            jax.ShapeDtypeStruct((1, length), F32),
        ],
        compiler_params=pltpu.CompilerParams(vmem_limit_bytes=VMEM_LIMIT),
        cost_estimate=pl.CostEstimate(
            flops=flops, bytes_accessed=8 * length * HEAD, transcendentals=length * length // 2
        ),
        name="attend",
    )(live[row], *queries, *keys, *values, seg_row, seg_col)


def attend_back_kernel(parts, block, live, *refs):
    q_in, k_in, v_in = refs[:parts], refs[parts : 2 * parts], refs[2 * parts : 3 * parts]
    g_in = refs[3 * parts : 4 * parts]
    seg_row, seg_col, mixed_ref, total_ref = refs[4 * parts : 4 * parts + 4]
    outs = refs[4 * parts + 4 : 5 * parts + 4]
    qs, ks, vs, gs, d_keys, d_values, d_query = refs[5 * parts + 4 :]
    at = pl.program_id(0)
    count = qs.shape[0] // block
    scale = 1.0 / math.sqrt(HEAD)

    @pl.when(at == 0)
    def _():
        gather_blocks(qs, q_in)
        gather_blocks(ks, k_in)
        gather_blocks(vs, v_in)
        gather_blocks(gs, g_in)
        d_keys[...] = jnp.zeros_like(d_keys)
        d_values[...] = jnp.zeros_like(d_values)

    here = pl.multiple_of(at * block, block)
    query = qs[pl.ds(here, block), :]
    grad = gs[pl.ds(here, block), :]
    seg_query = seg_row[:, pl.ds(here, block)]
    log_total = total_ref[:, pl.ds(here, block)]
    weighted = jnp.sum(
        mixed_ref[:, pl.ds(here, block)] * grad.astype(F32).T, axis=0, keepdims=True
    )
    d_query[...] = jnp.zeros_like(d_query)

    def back(step, masked):
        rows = pl.ds(pl.multiple_of(step * block, block), block)
        key, value = ks[rows, :], vs[rows, :]
        raw = dot(key, query, 1, 1) * (LOG2E / math.sqrt(HEAD))
        if masked:
            raw = jnp.where(seg_col[rows, 0:1] == seg_query, raw, NEGATIVE)
        probs = jnp.exp2(raw - log_total)
        d_scores = (probs * (dot(value, grad, 1, 1) - weighted)).astype(BF16)
        d_values[rows, :] += dot(probs.astype(BF16), grad, 1, 0)
        d_keys[rows, :] += dot(d_scores, query, 1, 0)
        d_query[...] += dot(d_scores, key, 0, 0)

    def step_of(step, carry):
        pl.when(live[at, step] == 1)(functools.partial(back, step, True))
        pl.when(live[at, step] == 2)(functools.partial(back, step, False))
        return carry

    lax.fori_loop(0, count, step_of, 0)
    low = (d_query[...] * scale).astype(BF16)
    per = count // parts
    size = per * block
    for slot, out in enumerate(outs):

        @pl.when(at // per == slot)
        def _(out=out):
            out[0, pl.ds(pl.multiple_of((at % per) * block, block), block), :] = low

    @pl.when(at == count - 1)
    def _():
        for slot, out in enumerate(outs):
            rows = slice(slot * size, (slot + 1) * size)
            out[1] = (d_keys[rows, :] * scale).astype(BF16)
            out[2] = d_values[rows, :].astype(BF16)


def attend_back(row, queries, keys, values, grads, seg_row, seg_col, live, mixed, totals):
    parts = len(queries)
    length = seg_row.shape[2]
    size = length // parts
    block = length // live.shape[1]
    part_spec = pl.BlockSpec((size, HEAD), lambda i, s: (row, 0))
    own_spec = pl.BlockSpec((size, HEAD), lambda i, s: (0, 0))
    whole = lambda i, s: (0, 0)
    return pl.pallas_call(
        functools.partial(attend_back_kernel, parts, block),
        grid_spec=pltpu.PrefetchScalarGridSpec(
            num_scalar_prefetch=1,
            grid=(length // block,),
            in_specs=[part_spec] * (3 * parts)
            + [own_spec] * parts
            + [
                pl.BlockSpec((None, 1, length), lambda i, s: (row, 0, 0)),
                pl.BlockSpec((None, length, HEAD), lambda i, s: (row, 0, 0)),
                pl.BlockSpec((HEAD, length), whole),
                pl.BlockSpec((1, length), whole),
            ],
            out_specs=[pl.BlockSpec((3, size, HEAD), lambda i, s: (0, 0, 0))] * parts,
            scratch_shapes=[pltpu.VMEM((length, HEAD), BF16)] * 4
            + [pltpu.VMEM((length, HEAD), F32)] * 2
            + [pltpu.VMEM((block, HEAD), F32)],
        ),
        out_shape=[jax.ShapeDtypeStruct((3, size, HEAD), BF16)] * parts,
        compiler_params=pltpu.CompilerParams(vmem_limit_bytes=VMEM_LIMIT),
        cost_estimate=pl.CostEstimate(
            flops=2 * 5 * length * length * HEAD * 5 // 8,
            bytes_accessed=16 * length * HEAD,
            transcendentals=length * length // 2,
        ),
        name="attend_back",
    )(live[row], *queries, *keys, *values, *grads, seg_row, seg_col, mixed, totals)


def normalize(hidden):
    center = hidden - jnp.mean(hidden, axis=-1, keepdims=True)
    inverse = lax.rsqrt(jnp.mean(center * center, axis=-1, keepdims=True) + EPSILON)
    return center * inverse, inverse


def normalize_back(grad, normal, inverse):
    return inverse * (
        grad
        - jnp.mean(grad, axis=-1, keepdims=True)
        - normal * jnp.mean(grad * normal, axis=-1, keepdims=True)
    )


def gelu_pair(pre):
    inner = 0.7978845608028654 * (pre + 0.044715 * pre * pre * pre)
    wave = jnp.tanh(inner)
    value = 0.5 * pre * (1.0 + wave)
    slope = 0.5 * (1.0 + wave) + 0.5 * pre * (1.0 - wave * wave) * 0.7978845608028654 * (
        1.0 + 3.0 * 0.044715 * pre * pre
    )
    return value, slope


def head_sum(part):
    half = part.shape[0] // 2
    near = core_swap(part[half:].astype(BF16))
    mine = (part[:half] + near.astype(F32)).astype(BF16)
    far = chip_swap(mine)
    return mine.astype(F32) + far.astype(F32)


def both_halves(value):
    return jnp.concatenate([value, core_swap(value)], axis=0)


def local(
    layer_input,
    segment_ids,
    qkv_weight,
    qv_bias,
    out_weight,
    out_bias,
    norm1_gain,
    norm1_bias,
    up_weight,
    up_bias,
    down_weight,
    down_bias,
    norm2_gain,
    norm2_bias,
    out_grad,
):
    rows, local_len, width = layer_input.shape
    fsdp, ctx = lax.axis_size("fsdp"), lax.axis_size("ctx")
    y, place = lax.axis_index("fsdp"), lax.axis_index("ctx")
    core = lax.axis_index("tp") % 2
    columns = qkv_weight.shape[2]
    heads = columns // HEAD
    half = local_len // 2
    share = width // fsdp
    assert heads == ctx == 4 and lax.axis_size("tp") == 4

    def features(value):
        return rotate(value, value.ndim - 1, y, fsdp)

    def features_back(value):
        return rotate(value, value.ndim - 1, (fsdp - y) % fsdp, fsdp)

    def spread(block):
        return [block] + [shift(block, "fsdp", -by) for by in range(1, fsdp)]

    own = [rotate(qkv_weight[:, j], 1, place, heads) for j in range(3)]
    query_blocks = spread(own[0])
    key_blocks = spread(after(own[1], *query_blocks[1:]))
    value_blocks = spread(after(own[2], *key_blocks[1:]))
    out_blocks = spread(after(rotate(out_weight, 0, place, heads), *value_blocks[1:]))
    up_blocks = spread(after(up_weight, *out_blocks[1:]))
    down_blocks = spread(after(down_weight, *up_blocks[1:]))

    x_all_rows = features(rotate(layer_input, 1, core, 2))
    x = x_all_rows.reshape(rows * local_len, width)
    biases = rotate(qv_bias, 1, place, heads)
    vectors = features(
        jnp.stack([out_bias, norm1_gain, norm1_bias, down_bias, norm2_gain, norm2_bias])
    ).astype(F32)
    out_shift, gain_one, shift_one, down_shift, gain_two, shift_two = (
        vectors[i : i + 1] for i in range(6)
    )
    upper = up_bias.astype(F32)[None]

    seg_own = rotate(segment_ids, 1, core, 2)
    seg = jnp.concatenate([seg_own] + [shift(seg_own, "ctx", by) for by in range(1, ctx)], axis=1)
    length = ctx * local_len
    seg_row = seg[:, None, :]
    seg_col = jnp.broadcast_to(seg[:, :, None], (rows, length, HEAD))
    blocks = seg.reshape(rows, length // half, half)
    low_id, high_id = blocks[:, :, 0], blocks[:, :, half - 1]
    meets = (low_id[:, :, None] <= high_id[:, None, :]) & (low_id[:, None, :] <= high_id[:, :, None])
    one = low_id == high_id
    same = one[:, :, None] & one[:, None, :] & meets
    live = meets.astype(jnp.int32) + same.astype(jnp.int32)

    zero_bias = jnp.zeros_like(biases[:1])

    def exchange(pieces):
        return [pieces[0]] + [shift(pieces[by], "ctx", by) for by in range(1, ctx)]

    def exchange_back(pieces):
        return [pieces[0]] + [shift(pieces[by], "ctx", -by) for by in range(1, ctx)]

    queries = exchange(project(x, query_blocks, biases[:1]))
    keys = exchange(project(x, key_blocks, zero_bias))
    values = exchange(project(x, value_blocks, biases[1:]))

    x_half = x_all_rows[:, :half].reshape(rows * half, width)
    x_ring = [after(x_half, *values[1:])]
    for _ in range(1, ctx):
        x_ring.append(shift(x_ring[-1], "ctx", 1))
    x_other = [core_swap(piece) for piece in x_ring[1:]]

    out_cat = jnp.concatenate(out_blocks, axis=1)
    up_cat = jnp.concatenate(up_blocks, axis=0)
    down_cat = jnp.concatenate(down_blocks, axis=1)

    attended, kept = [], []
    for r in range(rows):
        *pieces, mixed, totals = attend(r, queries, keys, values, seg_row, seg_col, live)
        kept.append((mixed, totals))
        attended.append(jnp.concatenate(exchange_back(pieces), axis=1))

    norm_one, normal_one, inverse_one, norm_low = [], [], [], []
    for r in range(rows):
        total = head_sum(dot(attended[r], out_cat, 1, 0))
        hidden = x_all_rows[r, :half].astype(F32) + total + out_shift
        normal, inverse = normalize(hidden)
        result = normal * gain_one + shift_one
        norm_one.append(result)
        normal_one.append(normal)
        inverse_one.append(inverse)
        norm_low.append(both_halves(result.astype(BF16)))

    act_low, slopes = [], []
    for r in range(rows):
        value, slope = gelu_pair(dot(norm_low[r], up_cat, 1, 0) + upper)
        act_low.append(value.astype(BF16))
        slopes.append(slope)

    grad_half = features(
        lax.dynamic_slice_in_dim(out_grad, core * half, half, axis=1)
    )
    layer_low, d_second, d_mlp_low, sums = [], [], [], []
    for r in range(rows):
        total = head_sum(dot(act_low[r], down_cat, 1, 0))
        normal, inverse = normalize(norm_one[r] + total + down_shift)
        layer_low.append(both_halves((normal * gain_two + shift_two).astype(BF16)))
        grad = grad_half[r].astype(F32)
        d_hidden = normalize_back(grad * gain_two, normal, inverse)
        low = d_hidden.astype(BF16)
        d_second.append(d_hidden)
        d_mlp_low.append(both_halves(low))
        sums.append(
            (jnp.sum(low.astype(F32), axis=0), jnp.sum(grad * normal, axis=0), jnp.sum(grad, axis=0))
        )

    d_pre_low = []
    for r in range(rows):
        d_act = dot(d_mlp_low[r], down_cat, 1, 1)
        d_pre_low.append((d_act * slopes[r]).astype(BF16))

    def reduced(lefts, rights, left_range, right_range, split_left, row_pieces, gate):
        def ranges(by, piece):
            if split_left:
                size = left_range // fsdp // row_pieces
                return ((by * row_pieces + piece) * size, size), (0, right_range)
            size = left_range // row_pieces
            return (piece * size, size), (by * (right_range // fsdp), right_range // fsdp)

        results = []
        for piece in range(row_pieces):
            arrived = None
            for by in range(1, fsdp):
                sent = weight_grad(lefts, rights, *ranges(by, piece))
                got = shift(after(sent, *gate), "fsdp", by)
                gate = [got]
                arrived = got if arrived is None else (arrived.astype(F32) + got.astype(F32))
            results.append(weight_grad(lefts, rights, *ranges(0, piece), add=arrived))
        return results, gate

    hidden_units = up_weight.shape[1]
    down_pieces, gate = reduced(act_low, d_mlp_low, hidden_units, width, False, 2, [])
    up_pieces, gate = reduced(norm_low, d_pre_low, width, hidden_units, True, 2, gate)

    d_first, d_attn_low = [], []
    for r in range(rows):
        d_norm = d_second[r] + head_sum(dot(d_pre_low[r], up_cat, 1, 1))
        d_hidden = normalize_back(d_norm * gain_one, normal_one[r], inverse_one[r])
        low = d_hidden.astype(BF16)
        d_first.append(d_hidden)
        d_attn_low.append(both_halves(low))
        sums[r] = sums[r] + (
            jnp.sum(low.astype(F32), axis=0),
            jnp.sum(d_norm * normal_one[r], axis=0),
            jnp.sum(d_norm, axis=0),
        )

    out_pieces, gate = reduced(attended, d_attn_low, columns, width, False, 1, gate)

    d_heads, d_joint = [], []
    for r in range(rows):
        d_att = dot(d_attn_low[r], out_cat, 1, 1).astype(BF16)
        grads = exchange([d_att[:, s * HEAD : (s + 1) * HEAD] for s in range(heads)])
        mixed, totals = kept[r]
        pieces = attend_back(
            r, queries, keys, values, grads, seg_row, seg_col, live, mixed, totals
        )
        d_heads.append(pieces)
        d_joint.append(exchange_back(pieces))

    flat_heads = [
        jnp.concatenate([d_heads[r][s][j] for j in range(3)], axis=1)
        for s in range(ctx)
        for r in range(rows)
    ]
    lefts = []
    for s in range(ctx):
        for r in range(rows):
            near = x_ring[s][r * half : (r + 1) * half]
            far = x_half_other(x_all_rows, x_other, s, r, half)
            lefts.append(jnp.concatenate([near, far], axis=0))
    joint_pieces, gate = reduced(lefts, flat_heads, width, 3 * HEAD, True, 1, gate)
    ring = [joint_pieces[0]]
    for _ in range(1, ctx):
        ring.append(shift(ring[-1], "ctx", 1))
    in_order = rotate(jnp.stack(ring[::-1]), 0, (ctx - 1 - place) % ctx, ctx)
    joint_grad = (
        in_order.reshape(ctx, share, 3, HEAD).transpose(1, 2, 0, 3).reshape(share, 3, columns)
    ).astype(F32)

    joint_cat = [
        jnp.concatenate([query_blocks[b], key_blocks[b], value_blocks[b]], axis=1)
        for b in range(fsdp)
    ]
    joint_cat = jnp.concatenate(joint_cat, axis=0)
    input_low = []
    bias_sums = 0.0
    for r in range(rows):
        d_row = jnp.concatenate(
            [d_joint[r][s][j] for j in range(3) for s in range(heads)], axis=1
        )
        bias_sums = bias_sums + jnp.sum(d_row.astype(F32), axis=0)
        total = head_sum(dot(d_row, joint_cat, 1, 1))
        input_low.append(both_halves((d_first[r] + total).astype(BF16)))

    layer_output = features_back(rotate(jnp.stack(layer_low), 1, core, 2))
    input_grad = features_back(rotate(jnp.stack(input_low), 1, core, 2)).astype(F32)

    wide = jnp.stack([sum(sums[r][i] for r in range(rows)) for i in range(6)])
    wide = features_back(wide)
    wide = wide + core_swap(wide)
    bias_rows = jnp.concatenate([bias_sums[None, :columns], bias_sums[None, 2 * columns :]], axis=0)
    bias_rows = rotate(bias_rows, 1, (heads - place) % heads, heads)
    up_sum = sum(jnp.sum(d_pre_low[r].astype(F32), axis=0) for r in range(rows))
    small = jnp.concatenate([wide.reshape(-1), up_sum, bias_rows.reshape(-1)])
    if fsdp == 2:
        small = small + shift(small, "fsdp", 1)
    else:
        small = lax.psum(small, "fsdp")
    small = small + lax.ppermute(small, "ctx", [(0, 1), (1, 0), (2, 3), (3, 2)])
    small = small + lax.ppermute(small, "ctx", [(0, 2), (2, 0), (1, 3), (3, 1)])
    wide = small[: 6 * width].reshape(6, width)
    up_bias_grad = small[6 * width : 6 * width + hidden_units]
    qv_bias_grad = small[6 * width + hidden_units :].reshape(2, columns)

    out_sum = rotate(out_pieces[0], 0, (heads - place) % heads, heads)
    down_sums = [line_sum(p) for p in down_pieces]
    up_sums = [line_sum(p) for p in up_pieces]
    out_total = line_sum(out_sum)
    return (
        layer_output,
        input_grad,
        joint_grad,
        qv_bias_grad,
        out_total.astype(F32),
        wide[3],
        wide[4],
        wide[5],
        jnp.concatenate(up_sums, axis=0).astype(F32),
        up_bias_grad,
        jnp.concatenate(down_sums, axis=0).astype(F32),
        wide[0],
        wide[1],
        wide[2],
    )


def x_half_other(x_all_rows, x_other, s, r, half):
    if s == 0:
        return x_all_rows[r, half:]
    return x_other[s - 1][r * half : (r + 1) * half]


def solution(mesh):
    return jax.shard_map(
        local,
        mesh=mesh,
        in_specs=(
            P("fsdp", "ctx", None),
            P("fsdp", "ctx"),
            P("fsdp", None, "tp"),
            P(None, "tp"),
            P("tp", "fsdp"),
            P(),
            P(),
            P(),
            P("fsdp", "tp"),
            P("tp"),
            P("tp", "fsdp"),
            P(),
            P(),
            P(),
            P("fsdp", "ctx", None),
        ),
        out_specs=(
            P("fsdp", "ctx", None),
            P("fsdp", "ctx", None),
            P("fsdp", None, "tp"),
            P(None, "tp"),
            P("tp", "fsdp"),
            P(),
            P(),
            P(),
            P("fsdp", "tp"),
            P("tp"),
            P("tp", "fsdp"),
            P(),
            P(),
            P(),
        ),
        check_vma=False,
    )
```

```python
import functools
import math

import jax
import jax.numpy as jnp
from jax import lax
from jax.experimental import pallas as pl
from jax.experimental.pallas import tpu as pltpu
from jax.sharding import PartitionSpec as P

HEAD = 128
EPSILON = 1e-12
NEGATIVE = -1e30
LOG2E = 1.4426950408889634
SCALE = 1.0 / math.sqrt(HEAD)
VMEM_LIMIT = 56 * 2**20

BF16 = jnp.bfloat16
F32 = jnp.float32


def dot(left, right, left_dim, right_dim):
    return lax.dot_general(
        left, right, (((left_dim,), (right_dim,)), ((), ())), preferred_element_type=F32
    )


def params():
    return pltpu.CompilerParams(vmem_limit_bytes=VMEM_LIMIT)


def cost(flops, moved, special=0):
    return pl.CostEstimate(flops=flops // 256, bytes_accessed=moved // 256, transcendentals=0)


def like(shape, dtype):
    return jax.ShapeDtypeStruct(shape, dtype)


def core_swap(value):
    size = lax.axis_size("tp")
    return lax.ppermute(value, "tp", [(i, i ^ 1) for i in range(size)])


def chip_swap(value):
    size = lax.axis_size("tp")
    return lax.ppermute(value, "tp", [(i, i ^ 2) for i in range(size)])


def shift(value, axis, by):
    size = lax.axis_size(axis)
    return lax.ppermute(value, axis, [(i, (i + by) % size) for i in range(size)])


def rotate(value, axis, by, count):
    size = value.shape[axis]
    block = size // count
    if count == 1:
        return value
    twice = jnp.concatenate([value, value], axis=axis)
    if count == 2:
        swapped = lax.slice_in_dim(twice, block, block + size, axis=axis)
        return jnp.where(by == 0, value, swapped)
    return lax.dynamic_slice_in_dim(twice, by * block, size, axis=axis)


def after(value, *others):
    return lax.optimization_barrier((value, *others))[0]


class Order:
    def __init__(self):
        self.last = ()

    def ready(self, value):
        return after(value, *self.last) if self.last else value

    def done(self, value):
        self.last = (value,)
        return value

    def pin(self, value):
        self.last += (value,)


class Weight:
    def __init__(self, parts, axis, blocks, rows=None):
        self.parts, self.axis, self.blocks = parts, axis, blocks
        self.turned = not isinstance(parts[0], tuple)
        self.shape = list((parts[0] if self.turned else parts[0][0]).shape[-2:])
        if self.turned:
            self.shape[axis] //= blocks
        if rows is not None:
            self.shape[0] = rows

    def arrays(self):
        if self.turned:
            return [self.parts[0]] * self.blocks
        return [array for array, _, _ in self.parts]

    def specs(self, split_axis, tile):
        shape = list(self.shape)
        steps = shape[split_axis] // tile
        shape[split_axis] = tile

        def spec(block):
            lead, row = (None, 0) if self.turned else self.parts[block][1:]

            def find(*args):
                at = [0, 0]
                if self.turned:
                    at[self.axis] = lax.rem(args[1][0] + block, self.blocks)
                else:
                    at[0] = row
                at[split_axis] = at[split_axis] * steps + args[0]
                return tuple(at) if lead is None else (lead, *at)

            return pl.BlockSpec(tuple(shape) if lead is None else (None, *shape), find)

        return [spec(b) for b in range(self.blocks)]


def grid_call(kernel, name, place, grid, in_specs, out_specs, out_shape, scratch, estimate, values):
    return pl.pallas_call(
        kernel,
        grid_spec=pltpu.PrefetchScalarGridSpec(
            num_scalar_prefetch=1,
            grid=grid,
            in_specs=in_specs,
            out_specs=out_specs,
            scratch_shapes=scratch,
        ),
        out_shape=out_shape,
        compiler_params=params(),
        cost_estimate=estimate,
        name=name,
    )(place, *values)


def fixed(shape):
    return pl.BlockSpec(shape, lambda i, p: (0,) * len(shape))


def project_kernel(blocks, x_ref, *refs):
    weights, bias_ref, out = refs[:blocks], *refs[blocks:]
    depth = x_ref.shape[1] // blocks
    acc = None
    for index, weight in enumerate(weights):
        part = dot(x_ref[:, index * depth : (index + 1) * depth], weight[...], 1, 0)
        acc = part if acc is None else acc + part
    low = (acc + bias_ref[...].astype(F32)).astype(BF16)
    for slot in range(out.shape[0]):
        out[slot] = low[:, slot * HEAD : (slot + 1) * HEAD]


def project(x, weight, bias):
    tokens, width = x.shape
    columns = weight.shape[1]
    heads = columns // HEAD
    tile = 256

    def whole(block):
        _, lead, row = weight.parts[block]
        return pl.BlockSpec((None, *weight.shape), lambda i: (lead, row, 0))

    return pl.pallas_call(
        functools.partial(project_kernel, weight.blocks),
        grid=(tokens // tile,),
        in_specs=[pl.BlockSpec((tile, width), lambda i: (i, 0))]
        + [whole(b) for b in range(weight.blocks)]
        + [pl.BlockSpec((1, columns), lambda i: (0, 0))],
        out_specs=pl.BlockSpec((heads, tile, HEAD), lambda i: (0, i, 0)),
        out_shape=like((heads, tokens, HEAD), BF16),
        compiler_params=params(),
        cost_estimate=cost(2 * tokens * width * columns, 2 * (tokens * width + width * columns)),
        name="project",
    )(x, *weight.arrays(), bias)


def up_kernel(blocks, place_ref, near, far, *refs):
    weights, bias_ref, act_ref, slope_ref = refs[:blocks], *refs[blocks:]
    half = near.shape[0]
    depth = near.shape[1] // blocks
    for index, source in enumerate((near, far)):
        pre = bias_ref[...].astype(F32)
        for block, weight in enumerate(weights):
            pre = pre + dot(source[:, block * depth : (block + 1) * depth], weight[...], 1, 0)
        square = pre * pre
        wave = jnp.tanh(pre * (0.7978845608028654 + 0.7978845608028654 * 0.044715 * square))
        half_up = 0.5 + 0.5 * wave
        slope = half_up + (0.5 * pre) * (1.0 - wave * wave) * (
            0.7978845608028654 + 3.0 * 0.7978845608028654 * 0.044715 * square
        )
        rows = slice(index * half, (index + 1) * half)
        act_ref[rows, :] = (pre * half_up).astype(BF16)
        slope_ref[rows, :] = slope.astype(slope_ref.dtype)


def up_project(place, near, far, weight, bias):
    half, width = near.shape
    columns = weight.shape[1]
    tile = 512
    out_spec = pl.BlockSpec((2 * half, tile), lambda i, p: (0, i))
    return grid_call(
        functools.partial(up_kernel, weight.blocks),
        "up_project",
        place,
        (columns // tile,),
        [fixed((half, width))] * 2
        + weight.specs(1, tile)
        + [pl.BlockSpec((1, tile), lambda i, p: (0, i))],
        [out_spec] * 2,
        [like((2 * half, columns), BF16)] * 2,
        [],
        cost(4 * half * width * columns, 2 * width * (2 * half + columns) + 8 * half * columns),
        [near, far, *weight.arrays(), bias],
    )


def act_back_kernel(blocks, place_ref, near, far, *refs):
    weights, slope_ref, out_ref, sum_ref = refs[:blocks], *refs[blocks:]
    half = near.shape[0]
    depth = near.shape[1] // blocks
    total = None
    for index, source in enumerate((near, far)):
        grad = None
        for block, weight in enumerate(weights):
            part = dot(source[:, block * depth : (block + 1) * depth], weight[...], 1, 1)
            grad = part if grad is None else grad + part
        rows = slice(index * half, (index + 1) * half)
        low = (grad * slope_ref[rows, :].astype(F32)).astype(BF16)
        out_ref[rows, :] = low
        part = jnp.sum(low.astype(F32), axis=0, keepdims=True)
        total = part if total is None else total + part
    sum_ref[...] = total


def act_back(place, near, far, weight, slope):
    half, width = near.shape
    columns = weight.shape[0]
    tile = 512
    out_spec = pl.BlockSpec((2 * half, tile), lambda i, p: (0, i))
    return grid_call(
        functools.partial(act_back_kernel, weight.blocks),
        "act_back",
        place,
        (columns // tile,),
        [fixed((half, width))] * 2 + weight.specs(0, tile) + [out_spec],
        [out_spec, pl.BlockSpec((1, tile), lambda i, p: (0, i))],
        [like((2 * half, columns), BF16), like((1, columns), F32)],
        [],
        cost(4 * half * width * columns, 2 * width * (2 * half + columns) + 8 * half * columns),
        [near, far, *weight.arrays(), slope],
    )


def head_back_kernel(blocks, place_ref, near, far, *refs):
    weights, out = refs[:blocks], refs[blocks]
    half = near.shape[0]
    depth = near.shape[1] // blocks
    for index, source in enumerate((near, far)):
        grad = None
        for block, weight in enumerate(weights):
            part = dot(source[:, block * depth : (block + 1) * depth], weight[...], 1, 1)
            grad = part if grad is None else grad + part
        low = grad.astype(BF16)
        for slot in range(out.shape[0]):
            out[slot, index * half : (index + 1) * half, :] = low[:, slot * HEAD : (slot + 1) * HEAD]


def head_back(place, near, far, weight):
    half, width = near.shape
    columns = weight.shape[0]
    heads = columns // HEAD
    return grid_call(
        functools.partial(head_back_kernel, weight.blocks),
        "head_back",
        place,
        (1,),
        [fixed((half, width))] * 2 + weight.specs(0, columns),
        fixed((heads, 2 * half, HEAD)),
        like((heads, 2 * half, HEAD), BF16),
        [],
        cost(4 * half * width * columns, 2 * width * (2 * half + columns)),
        [near, far, *weight.arrays()],
    )


def terms_kernel(transposed, blocks, parts, place_ref, left_ref, *refs):
    weights = refs[: blocks * parts]
    sent, kept, *rest = refs[blocks * parts :]
    at = pl.program_id(0)
    left = left_ref
    if rest:
        left = rest[0]

        @pl.when(at == 0)
        def _():
            if len(left_ref.shape) == 3:
                for head in range(left_ref.shape[0]):
                    left[:, head * HEAD : (head + 1) * HEAD] = left_ref[head]
            else:
                heads, kinds = left_ref.shape[:2]
                for head in range(heads):
                    for kind in range(kinds):
                        column = (kind * heads + head) * HEAD
                        left[:, column : column + HEAD] = left_ref[head, kind]
                rest[1][...] = jnp.sum(left[...].astype(F32), axis=0, keepdims=True)

    half = sent.shape[0]
    depth = left.shape[1] // parts
    share = sent.shape[1] // blocks
    for block in range(blocks):
        acc = None
        for part in range(parts):
            weight = weights[part * blocks + block]
            here = dot(
                left[:, part * depth : (part + 1) * depth], weight[...], 1, 1 if transposed else 0
            )
            acc = here if acc is None else acc + here
        tile = acc.shape[1]
        columns = pl.ds(pl.multiple_of(block * share + at * tile, tile), tile)
        kept[:, columns] = acc[:half]
        sent[:, columns] = acc[half:].astype(BF16)


def terms(place, left, weights, transposed, tile):
    tokens = left.shape[-2]
    blocks, parts = weights[0].blocks, len(weights)
    out_axis = 0 if transposed else 1
    share = weights[0].shape[out_axis]
    tile = min(tile, share)
    depth = math.prod(left.shape) // tokens
    half = tokens // 2
    outs = [like((half, blocks * share), BF16), like((half, blocks * share), F32)]
    if left.ndim > 2:
        outs.append(like((tokens, depth), BF16))
    if left.ndim > 3:
        outs.append(like((1, depth), F32))
    return grid_call(
        functools.partial(terms_kernel, transposed, blocks, parts),
        "terms",
        place,
        (share // tile,),
        [fixed(left.shape)] + [spec for w in weights for spec in w.specs(out_axis, tile)],
        [fixed(v.shape) for v in outs],
        outs,
        [],
        cost(
            2 * tokens * depth * blocks * share,
            2 * depth * (tokens + blocks * share) + 6 * half * blocks * share,
        ),
        [left] + [v for w in weights for v in w.arrays()],
    )


def grad_kernel(pairs, place_ref, *refs):
    out = refs[-1]
    acc = None
    for index in range(pairs):
        part = dot(refs[2 * index][...], refs[2 * index + 1][...], 0, 0)
        acc = part if acc is None else acc + part
    out[...] = acc.astype(out.dtype)


def weight_grad(pairs, rows, columns, place, blocks, split_left):
    row_from, row_count = rows
    col_from, col_count = columns
    row_tile = min(1024, row_count // blocks if split_left else row_count)
    col_tile = min(512, col_count if split_left else col_count // blocks)
    row_base, col_base = row_from // row_tile, col_from // col_tile
    specs, values, depth = [], [], 0
    row_per, col_per = row_count // blocks // row_tile, col_count // blocks // col_tile

    def turned(at, per, place_ref):
        return lax.rem(at // per + blocks - place_ref[0], blocks) * per + lax.rem(at, per)

    def left_map(first):
        if split_left:
            return lambda i, j, p: (first, turned(i, row_per, p))
        return lambda i, j, p: (first, i + row_base)

    def right_map(first):
        if split_left:
            return lambda i, j, p: (first, j + col_base)
        return lambda i, j, p: (first, turned(j, col_per, p))

    for (left, left_at), (right, right_at), height in pairs:
        specs.append(pl.BlockSpec((height, row_tile), left_map(left_at)))
        specs.append(pl.BlockSpec((height, col_tile), right_map(right_at)))
        values += [left, right]
        depth += height
    return pl.pallas_call(
        functools.partial(grad_kernel, len(pairs)),
        grid_spec=pltpu.PrefetchScalarGridSpec(
            num_scalar_prefetch=1,
            grid=(row_count // row_tile, col_count // col_tile),
            in_specs=specs,
            out_specs=pl.BlockSpec((row_tile, col_tile), lambda i, j, p: (i, j)),
        ),
        out_shape=like((row_count, col_count), BF16),
        compiler_params=params(),
        cost_estimate=cost(
            2 * row_count * col_count * depth,
            2 * (depth * row_count + depth * col_count + row_count * col_count),
        ),
        name="weight_grad",
    )(place, *values)


def joint_grad_kernel(rows, count, has_add, place_ref, *refs):
    heads, near, far = refs[:rows], refs[rows : rows + count], refs[rows + count : rows + 2 * count]
    out, scratch = refs[-2:]
    _, kinds, size, _ = heads[0].shape
    half = size // 2
    depth = rows * half

    @pl.when(pl.program_id(0) == 0)
    def _():
        for step in range(count):
            source = lax.rem(place_ref[0] + count - step, count)
            for row, head in enumerate(heads):
                for part in range(2):
                    start = ((step * 2 + part) * rows + row) * half
                    for kind in range(kinds):
                        scratch[start : start + half, kind * HEAD : (kind + 1) * HEAD] = head[
                            source, kind, part * half : (part + 1) * half, :
                        ]

    acc = None
    for index in range(2 * count):
        left = (near, far)[index % 2][index // 2]
        part = dot(left[...], scratch[index * depth : (index + 1) * depth, :], 0, 0)
        acc = part if acc is None else acc + part
    if has_add:
        acc = acc + refs[rows + 2 * count][...].astype(F32)
    out[...] = acc.astype(BF16)


def joint_grad_terms(place, near, far, heads, left_cols, add=None):
    row_from, rows = left_cols
    tile = min(256, rows)
    base = row_from // tile
    places, kinds, size, _ = heads[0].shape
    depth = near[0].shape[0]
    specs = [pl.BlockSpec(h.shape, lambda i, p: (0, 0, 0, 0)) for h in heads]
    specs += [pl.BlockSpec((depth, tile), lambda i, p: (0, i + base))] * (2 * places)
    values = [*heads, *near, *far]
    if add is not None:
        specs.append(pl.BlockSpec((tile, kinds * HEAD), lambda i, p: (i, 0)))
        values.append(add)
    return pl.pallas_call(
        functools.partial(joint_grad_kernel, len(heads), places, add is not None),
        grid_spec=pltpu.PrefetchScalarGridSpec(
            num_scalar_prefetch=1,
            grid=(rows // tile,),
            in_specs=specs,
            out_specs=pl.BlockSpec((tile, kinds * HEAD), lambda i, p: (i, 0)),
            scratch_shapes=[pltpu.VMEM((2 * places * depth, kinds * HEAD), BF16)],
        ),
        out_shape=like((rows, kinds * HEAD), BF16),
        compiler_params=params(),
        cost_estimate=cost(
            4 * places * depth * rows * kinds * HEAD, 4 * places * depth * (rows + kinds * HEAD)
        ),
        name="joint_grad",
    )(place, *values)


def gather_blocks(scratch, source, transposed=False):
    count, size, _ = source.shape
    for index in range(count):
        rows = slice(index * size, (index + 1) * size)
        if transposed:
            scratch[:, rows] = source[index].T
        else:
            scratch[rows, :] = source[index]


def put_rows(out, at, query_block, value, lead=()):
    size = out.shape[-2]
    per = query_block // size
    for slot in range(per):
        out[(at * per + slot, *lead)] = value[slot * size : (slot + 1) * size]


def attend_kernel(query_block, key_block, live, *refs):
    q_in, k_in, v_in, seg_row, seg_col, out, mixed_ref, total_ref = refs[:8]
    qs, ks, vs, scores, top, total, mixed = refs[8:]
    at = pl.program_id(0)
    count = qs.shape[0] // key_block

    @pl.when(at == 0)
    def _():
        gather_blocks(qs, q_in)
        gather_blocks(ks, k_in)
        gather_blocks(vs, v_in)

    here = pl.ds(pl.multiple_of(at * query_block, query_block), query_block)
    query = qs[here, :]
    seg_query = seg_row[:, here]
    top[...] = jnp.full_like(top, NEGATIVE)
    total[...] = jnp.zeros_like(total)
    mixed[...] = jnp.zeros_like(mixed)

    def score(step, masked):
        rows = pl.ds(pl.multiple_of(step * key_block, key_block), key_block)
        raw = dot(ks[rows, :], query, 1, 1) * (LOG2E * SCALE)
        if masked:
            raw = jnp.where(seg_col[rows, 0:1] == seg_query, raw, NEGATIVE)
        scores[rows, :] = raw
        top[...] = jnp.maximum(top[...], jnp.max(raw, axis=0, keepdims=True))

    def first(step, carry):
        pl.when(live[at, step] == 1)(functools.partial(score, step, True))
        pl.when(live[at, step] == 2)(functools.partial(score, step, False))
        return carry

    def second(step, carry):
        @pl.when(live[at, step] > 0)
        def _():
            rows = pl.ds(pl.multiple_of(step * key_block, key_block), key_block)
            weight = jnp.exp2(scores[rows, :] - top[...])
            total[...] += jnp.sum(weight, axis=0, keepdims=True)
            mixed[...] += dot(vs[rows, :], weight.astype(BF16), 0, 0)

        return carry

    lax.fori_loop(0, count, first, 0)
    lax.fori_loop(0, count, second, 0)
    result = mixed[...] / total[...]
    mixed_ref[:, here] = result
    total_ref[:, here] = top[...] + jnp.log2(total[...])
    put_rows(out, at, query_block, result.T.astype(BF16))


def attend(row, queries, keys, values, seg_row, seg_col, live):
    parts = queries.shape[0]
    length = seg_row.shape[2]
    size = length // parts
    query_block, key_block = length // live.shape[1], length // live.shape[2]
    part_spec = pl.BlockSpec((parts, size, HEAD), lambda i, s: (0, row, 0))
    whole = lambda i, s: (0, 0)
    return pl.pallas_call(
        functools.partial(attend_kernel, query_block, key_block),
        grid_spec=pltpu.PrefetchScalarGridSpec(
            num_scalar_prefetch=1,
            grid=(length // query_block,),
            in_specs=[
                part_spec,
                part_spec,
                part_spec,
                pl.BlockSpec((None, 1, length), lambda i, s: (row, 0, 0)),
                pl.BlockSpec((None, length, HEAD), lambda i, s: (row, 0, 0)),
            ],
            out_specs=[
                pl.BlockSpec((parts, size, HEAD), lambda i, s: (0, 0, 0)),
                pl.BlockSpec((HEAD, length), whole),
                pl.BlockSpec((1, length), whole),
            ],
            scratch_shapes=[pltpu.VMEM((length, HEAD), BF16)] * 3
            + [
                pltpu.VMEM((length, query_block), F32),
                pltpu.VMEM((1, query_block), F32),
                pltpu.VMEM((1, query_block), F32),
                pltpu.VMEM((HEAD, query_block), F32),
            ],
        ),
        out_shape=[
            like((parts, size, HEAD), BF16),
            like((HEAD, length), F32),
            like((1, length), F32),
        ],
        compiler_params=params(),
        cost_estimate=cost(4 * length * length * HEAD, 8 * length * HEAD, length * length // 2),
        name="attend",
    )(live[row], queries, keys, values, seg_row, seg_col)


def attend_back_kernel(query_block, key_block, live, *refs):
    q_in, k_in, v_in, g_in, seg_row, seg_col, mixed_ref, total_ref, out = refs[:9]
    qs, ks, vs, gs, kt, d_keys, d_values, d_query = refs[9:]
    at = pl.program_id(0)
    count = qs.shape[0] // key_block

    @pl.when(at == 0)
    def _():
        gather_blocks(qs, q_in)
        gather_blocks(ks, k_in)
        gather_blocks(vs, v_in)
        gather_blocks(gs, g_in)
        gather_blocks(kt, k_in, True)
        d_keys[...] = jnp.zeros_like(d_keys)
        d_values[...] = jnp.zeros_like(d_values)

    here = pl.ds(pl.multiple_of(at * query_block, query_block), query_block)
    query = qs[here, :]
    grad = gs[here, :]
    seg_query = seg_row[:, here]
    log_total = total_ref[:, here]
    weighted = jnp.sum(mixed_ref[:, here] * grad.astype(F32).T, axis=0, keepdims=True)
    d_query[...] = jnp.zeros_like(d_query)

    def back(step, masked):
        rows = pl.ds(pl.multiple_of(step * key_block, key_block), key_block)
        key, value = ks[rows, :], vs[rows, :]
        raw = dot(key, query, 1, 1) * (LOG2E * SCALE)
        if masked:
            raw = jnp.where(seg_col[rows, 0:1] == seg_query, raw, NEGATIVE)
        probs = jnp.exp2(raw - log_total)
        d_scores = (probs * (dot(value, grad, 1, 1) - weighted)).astype(BF16)
        d_values[rows, :] += dot(probs.astype(BF16), grad, 1, 0)
        d_keys[rows, :] += dot(d_scores, query, 1, 0)
        d_query[...] += dot(kt[:, rows], d_scores, 1, 0)

    def step_of(step, carry):
        pl.when(live[at, step] == 1)(functools.partial(back, step, True))
        pl.when(live[at, step] == 2)(functools.partial(back, step, False))
        return carry

    lax.fori_loop(0, count, step_of, 0)
    put_rows(out, at, query_block, (d_query[...] * SCALE).T.astype(BF16), (0,))

    @pl.when(at == pl.num_programs(0) - 1)
    def _():
        size = out.shape[2]
        for slot in range(out.shape[0]):
            rows = slice(slot * size, (slot + 1) * size)
            out[slot, 1] = (d_keys[rows, :] * SCALE).astype(BF16)
            out[slot, 2] = d_values[rows, :].astype(BF16)


def attend_back(row, queries, keys, values, grads, seg_row, seg_col, live, mixed, totals):
    parts = queries.shape[0]
    length = seg_row.shape[2]
    size = length // parts
    query_block, key_block = length // live.shape[1], length // live.shape[2]
    part_spec = pl.BlockSpec((parts, size, HEAD), lambda i, s: (0, row, 0))
    whole = lambda i, s: (0, 0)
    return pl.pallas_call(
        functools.partial(attend_back_kernel, query_block, key_block),
        grid_spec=pltpu.PrefetchScalarGridSpec(
            num_scalar_prefetch=1,
            grid=(length // query_block,),
            in_specs=[
                part_spec,
                part_spec,
                part_spec,
                pl.BlockSpec((parts, size, HEAD), lambda i, s: (0, 0, 0)),
                pl.BlockSpec((None, 1, length), lambda i, s: (row, 0, 0)),
                pl.BlockSpec((None, length, HEAD), lambda i, s: (row, 0, 0)),
                pl.BlockSpec((HEAD, length), whole),
                pl.BlockSpec((1, length), whole),
            ],
            out_specs=pl.BlockSpec((parts, 3, size, HEAD), lambda i, s: (0, 0, 0, 0)),
            scratch_shapes=[pltpu.VMEM((length, HEAD), BF16)] * 4
            + [pltpu.VMEM((HEAD, length), BF16)]
            + [pltpu.VMEM((length, HEAD), F32)] * 2
            + [pltpu.VMEM((HEAD, query_block), F32)],
        ),
        out_shape=like((parts, 3, size, HEAD), BF16),
        compiler_params=params(),
        cost_estimate=cost(10 * length * length * HEAD, 16 * length * HEAD, length * length // 2),
        name="attend_back",
    )(live[row], queries, keys, values, grads, seg_row, seg_col, mixed, totals)


def normalize(hidden):
    center = hidden - jnp.mean(hidden, axis=-1, keepdims=True)
    inverse = lax.rsqrt(jnp.mean(center * center, axis=-1, keepdims=True) + EPSILON)
    return center * inverse, inverse


def normalize_back(grad, normal, inverse):
    return inverse * (
        grad
        - jnp.mean(grad, axis=-1, keepdims=True)
        - normal * jnp.mean(grad * normal, axis=-1, keepdims=True)
    )


def add_up(ref, values):
    @pl.when(pl.program_id(0) == 0)
    def _():
        ref[...] = jnp.zeros_like(ref)

    ref[...] += jnp.concatenate([jnp.sum(v, axis=0, keepdims=True) for v in values], axis=0)


def norm_one_kernel(near, far, x, vectors, normal_ref, inverse_ref, low_ref):
    hidden = x[...].astype(F32) + (near[...].astype(F32) + far[...].astype(F32)) + vectors[0:1, :]
    normal, inverse = normalize(hidden)
    normal_ref[...] = normal
    inverse_ref[...] = jnp.broadcast_to(inverse, inverse_ref.shape)
    low_ref[...] = (normal * vectors[1:2, :] + vectors[2:3, :]).astype(BF16)


def norm_two_kernel(near, far, normal_one, grad_ref, vectors, out_ref, second_ref, low_ref, sum_ref):
    hidden = (
        normal_one[...] * vectors[1:2, :]
        + vectors[2:3, :]
        + (near[...].astype(F32) + far[...].astype(F32))
        + vectors[3:4, :]
    )
    normal, inverse = normalize(hidden)
    out_ref[...] = (normal * vectors[4:5, :] + vectors[5:6, :]).astype(BF16)
    grad = grad_ref[...].astype(F32)
    d_hidden = normalize_back(grad * vectors[4:5, :], normal, inverse)
    low = d_hidden.astype(BF16)
    second_ref[...] = d_hidden
    low_ref[...] = low
    add_up(sum_ref, (low.astype(F32), grad * normal, grad))


def norm_back_kernel(near, far, second, normal_ref, inverse_ref, vectors, first_ref, low_ref, sum_ref):
    d_norm = second[...] + (near[...].astype(F32) + far[...].astype(F32))
    normal = normal_ref[...]
    d_hidden = normalize_back(d_norm * vectors[1:2, :], normal, inverse_ref[:, 0:1])
    low = d_hidden.astype(BF16)
    first_ref[...] = d_hidden
    low_ref[...] = low
    add_up(sum_ref, (low.astype(F32), d_norm * normal, d_norm))


def by_tokens(kernel, name, inputs, vectors, outs, sums=0):
    tokens, width = inputs[0][0].shape
    tile = tokens // 4
    specs = [
        pl.BlockSpec((tile, v.shape[1]), lambda i, a=at: (a * 4 + i, 0)) for v, at in inputs
    ]
    out_specs = [pl.BlockSpec((tile, columns), lambda i: (i, 0)) for columns, _ in outs]
    out_shape = [like((tokens, columns), dtype) for columns, dtype in outs]
    if sums:
        out_specs.append(pl.BlockSpec((sums, width), lambda i: (0, 0)))
        out_shape.append(like((sums, width), F32))
    return pl.pallas_call(
        kernel,
        grid=(4,),
        in_specs=specs + [pl.BlockSpec(vectors.shape, lambda i: (0, 0))],
        out_specs=out_specs,
        out_shape=out_shape,
        compiler_params=params(),
        cost_estimate=cost(20 * tokens * width, 16 * tokens * width),
        name=name,
    )(*[v for v, _ in inputs], vectors)


def local(
    layer_input,
    segment_ids,
    qkv_weight,
    qv_bias,
    out_weight,
    out_bias,
    norm1_gain,
    norm1_bias,
    up_weight,
    up_bias,
    down_weight,
    down_bias,
    norm2_gain,
    norm2_bias,
    out_grad,
):
    rows, local_len, width = layer_input.shape
    fsdp, ctx = lax.axis_size("fsdp"), lax.axis_size("ctx")
    y, place = lax.axis_index("fsdp"), lax.axis_index("ctx")
    core = lax.axis_index("tp") % 2
    columns = qkv_weight.shape[2]
    hidden_units = up_weight.shape[1]
    heads = columns // HEAD
    half = local_len // 2
    share = width // fsdp
    each = range(rows)
    assert heads == ctx == 4 and lax.axis_size("tp") == 4
    order = Order()

    def features(value):
        return rotate(value, value.ndim - 1, y, fsdp)

    def features_back(value):
        return rotate(value, value.ndim - 1, (fsdp - y) % fsdp, fsdp)

    def spread(block):
        return [block] + [shift(block, "fsdp", -by) for by in range(1, fsdp)]

    def swap_ctx(value):
        return lax.all_to_all(value, "ctx", 0, 0, tiled=True)

    def from_all(value):
        return swap_ctx(jnp.broadcast_to(value[None], (ctx, *value.shape)))

    def both(value):
        return value, core_swap(value)

    seg_own = rotate(segment_ids, 1, core, 2)
    seg = from_all(seg_own).transpose(1, 0, 2).reshape(rows, ctx * local_len)

    x_rows = features(rotate(layer_input, 1, core, 2))
    x = x_rows.reshape(rows * local_len, width)

    vectors = features(
        jnp.stack([out_bias, norm1_gain, norm1_bias, down_bias, norm2_gain, norm2_bias])
    ).astype(F32)
    grad_half = features(
        lax.dynamic_slice_in_dim(out_grad, core * half, half, axis=1)
    ).reshape(rows * half, width)

    zero_bias = jnp.zeros_like(qv_bias[:1])
    biases = qv_bias[:1], zero_bias, qv_bias[1:]
    pair = spread(jnp.stack([qkv_weight[:, 0], qkv_weight[:, 1]]))
    cuts = share // columns
    pieces = [out_weight[:, i * columns : (i + 1) * columns] for i in range(cuts)]
    rest = jnp.concatenate([qkv_weight[:, 2], *pieces], axis=0)
    rest, seg, *pair[1:] = lax.optimization_barrier((rest, seg, *pair[1:]))
    rest = [v[None] for v in spread(after(rest, x))]
    joint_matrices = [
        Weight([(v, 0, 0) for v in pair], 0, fsdp),
        Weight([(v, 1, 0) for v in pair], 0, fsdp),
        Weight([(v, 0, 0) for v in rest], 0, fsdp, share),
    ]
    if cuts:
        out_parts = [(v, 0, cuts + i) for v in rest for i in range(cuts)]
        out_full = Weight(out_parts, 1, fsdp * cuts, columns)
    else:
        out_full = Weight([(v, None, 0) for v in spread(after(out_weight, rest[1]))], 1, fsdp)
    query_pieces = project(x, joint_matrices[0], biases[0])
    queries = swap_ctx(query_pieces)
    key_pieces = project(after(x, query_pieces), joint_matrices[1], biases[1])
    keys = swap_ctx(after(key_pieces, queries))
    gate = [*rest[1:], keys]

    def whole(block, axis):
        full = lax.all_gather(after(block, *gate), "fsdp", axis=axis, tiled=True)
        return Weight([full], axis, fsdp)

    up_full = whole(up_weight, 0)
    down_full = whole(down_weight, 1)
    pieces = order.done(project(after(x, key_pieces), joint_matrices[2], biases[2]))
    values = swap_ctx(after(pieces, keys))
    fsdp_place = y.astype(jnp.int32)[None]

    length = ctx * local_len
    seg_row = seg[:, None, :]
    seg_col = jnp.broadcast_to(seg[:, :, None], (rows, length, HEAD))

    def span(size):
        blocks = seg.reshape(rows, length // size, size)
        return jnp.min(blocks, axis=2), jnp.max(blocks, axis=2)

    (query_low, query_high), (key_low, key_high) = span(2 * local_len), span(local_len)
    meets = (query_low[:, :, None] <= key_high[:, None, :]) & (
        key_low[:, None, :] <= query_high[:, :, None]
    )
    same = (query_low == query_high)[:, :, None] & (key_low == key_high)[:, None, :] & meets
    live = meets.astype(jnp.int32) + same.astype(jnp.int32)

    attended, kept = [], []
    for r in each:
        pieces, mixed, totals = attend(
            r, order.ready(queries), keys, values, seg_row, seg_col, live
        )
        order.done(totals)
        kept.append((mixed, totals))
        attended.append(swap_ctx(pieces))

    def begin(left, weights, transposed, tile):
        sent, mine, *rest = terms(fsdp_place, order.ready(left), weights, transposed, tile)
        order.done(sent)
        return core_swap(sent), mine, *rest

    def middle(near, mine):
        total = order.done((order.ready(mine) + near.astype(F32)).astype(BF16))
        return total, chip_swap(total)

    parts = [begin(attended[r], [out_full], False, 512) for r in each]
    attended_last = attended[-1]
    attended = [parts[r][2] for r in each]
    totals = [middle(*parts[r][:2]) for r in each]

    x_near = [after(x_rows[:, :half].reshape(rows * half, width), attended_last)]
    x_near.append(shift(x_near[0], "ctx", 1))

    normal_one, inverse_one, norm_low = [], [], []
    for r in each:
        near, far = totals[r]
        normal, inverse, low = by_tokens(
            norm_one_kernel,
            "norm_one",
            [(order.ready(near), 0), (far, 0), (x, 2 * r)],
            vectors,
            [(width, F32), (HEAD, F32), (width, BF16)],
        )
        order.done(low)
        normal_one.append(normal)
        inverse_one.append(inverse)
        norm_low.append(both(low))

    act_low, slopes = [], []
    for r in each:
        near, far = norm_low[r]
        if r == 0:
            x_near.append(shift(order.ready(x_near[1]), "ctx", 1))
        act, slope = up_project(fsdp_place, order.ready(near), far, up_full, up_bias[None])
        order.done(act)
        act_low.append(act)
        slopes.append(slope)

    order.pin(x_near[2])
    x_near.append(shift(x_near[2], "ctx", 1))
    parts = [begin(act_low[r], [down_full], False, 512) for r in each]
    totals = [middle(*parts[r]) for r in each]

    layer_low, second, mlp_low, sums_two = [], [], [], []
    pre_low, up_sums, up_parts = [], [], []

    def norm_two(r):
        near, far = totals[r]
        out, d_second, low, sums = by_tokens(
            norm_two_kernel,
            "norm_two",
            [(order.ready(near), 0), (far, 0), (normal_one[r], 0), (grad_half, r)],
            vectors,
            [(width, BF16), (width, F32), (width, BF16)],
            3,
        )
        order.done(low)
        layer_low.append(out)
        second.append(d_second)
        mlp_low.append(both(low))
        sums_two.append(sums)

    def act_step(r):
        near, far = mlp_low[r]
        low, sums = act_back(fsdp_place, order.ready(near), far, down_full, slopes[r])
        order.done(low)
        pre_low.append(low)
        up_sums.append(sums)

    def up_step(r):
        up_parts.append(begin(pre_low[r], [up_full], True, 512))

    halves = range(2)
    gradients = {}

    def pairs_of(left, right):
        made = []
        for r in each:
            for h in halves:
                a = (left[r][h], 0) if isinstance(left[r], tuple) else (left[r], h)
                b = (right[r][h], 0) if isinstance(right[r], tuple) else (right[r], h)
                made.append((a, b, half))
        return made

    def give(name, pairs, shape, split_left, piece, pieces):
        (left, *others) = pairs
        left = ((order.ready(left[0][0]), left[0][1]), *left[1:])
        if split_left:
            part = shape[1] // pieces
            ranges = (0, shape[0]), (piece * part, part)
        else:
            part = shape[0] // pieces
            ranges = (piece * part, part), (0, shape[1])
        mine = order.done(
            weight_grad([left, *others], *ranges, fsdp_place, fsdp, split_left)
        )
        gradients[name, piece] = lax.psum_scatter(
            mine, "fsdp", scatter_dimension=0 if split_left else 1, tiled=True
        )

    def line_one(value):
        return value, lax.ppermute(value, "ctx", [(0, 1), (3, 2)])

    def line_two(value, other):
        pair = order.done((order.ready(value).astype(F32) + other.astype(F32)).astype(BF16))
        return pair, lax.ppermute(pair, "ctx", [(1, 2), (2, 1)])

    def line_three(pair, other):
        total = order.done((order.ready(pair).astype(F32) + other.astype(F32)).astype(BF16))
        return total, lax.ppermute(total, "ctx", [(1, 0), (2, 3)])

    outer = (place == 0) | (place == ctx - 1)

    def line_end(total, other):
        return jnp.where(outer, other, total)

    first, attn_low, sums_one, head_grads = [], [], [], []

    def norm_back(r):
        near, far = up_totals[r]
        d_first, low, sums = by_tokens(
            norm_back_kernel,
            "norm_back",
            [(order.ready(near), 0), (far, 0), (second[r], 0), (normal_one[r], 0), (inverse_one[r], 0)],
            vectors,
            [(width, F32), (width, BF16)],
            3,
        )
        order.done(low)
        first.append(d_first)
        attn_low.append(both(low))
        sums_one.append(sums)

    def head_step(r):
        near, far = attn_low[r]
        pieces = order.done(head_back(fsdp_place, order.ready(near), far, out_full))
        head_grads.append(swap_ctx(pieces))

    joint_back, joint_rows = [], []

    def attend_step(r):
        mixed, row_totals = kept[r]
        grads = order.ready(head_grads[r])
        pieces = attend_back(
            r, queries, keys, values, grads, seg_row, seg_col, live, mixed, row_totals
        )
        joint_back.append(order.done(pieces))
        joint_rows.append(swap_ctx(pieces))

    lined = {}

    def line_start(name, piece):
        lined[name, piece] = line_one(order.ready(gradients[name, piece]))

    def line_step(step, name, piece):
        lined[name, piece] = step(*lined[name, piece])

    def small_start(value):
        value = value + shift(value, "fsdp", 1) if fsdp == 2 else lax.psum(value, "fsdp")
        value = order.done(value)
        return value, lax.ppermute(value, "ctx", [(0, 1), (1, 0), (2, 3), (3, 2)])

    def small_step(value, other):
        value = order.done(order.ready(value) + other)
        return value, lax.ppermute(value, "ctx", [(0, 2), (2, 0), (1, 3), (3, 1)])

    def small_end(value, other):
        return order.done(order.ready(value) + other)

    norm_two(0)
    act_step(0)
    up_step(0)
    order.pin(x_near[3])
    norm_two(1)
    up_totals = [middle(*up_parts[0])]
    down_args = (pairs_of(act_low, mlp_low), (hidden_units, width), False)
    give("down", *down_args, 0, 2)
    act_step(1)
    up_step(1)
    give("down", *down_args, 1, 2)
    up_totals.append(middle(*up_parts[1]))
    up_args = (pairs_of(norm_low, pre_low), (width, hidden_units), True)
    norm_back(0)
    give("up", *up_args, 0, 2)
    head_step(0)
    line_start("down", 0)
    norm_back(1)
    give("up", *up_args, 1, 2)
    head_step(1)
    out_args = (pairs_of(attended, attn_low), (columns, width), False)
    give("out", *out_args, 0, 1)
    wide = features_back(jnp.concatenate([sum(sums_two), sum(sums_one)], axis=0))
    wide = wide + core_swap(wide)
    line_step(line_two, "down", 0)
    line_start("down", 1)
    attend_step(0)
    wide_small = small_start(jnp.concatenate([wide.reshape(-1), sum(up_sums).reshape(-1)]))
    attend_step(1)

    x_far = [x_rows[:, half:].reshape(rows * half, width)] + [core_swap(v) for v in x_near[1:]]
    ctx_place = place.astype(jnp.int32)[None]
    arrived = None
    for by in range(1, fsdp):
        sent = joint_grad_terms(
            ctx_place, [order.ready(x_near[0])] + x_near[1:], x_far, joint_back, (by * share, share)
        )
        got = shift(order.done(sent), "fsdp", by)
        arrived = got if arrived is None else (arrived.astype(F32) + got.astype(F32))

    line_step(line_three, "down", 0)
    line_step(line_two, "down", 1)
    line_start("up", 0)
    wide_small = small_step(*wide_small)
    in_parts = [begin(joint_rows[0], joint_matrices, True, 512)]
    mine = joint_grad_terms(
        ctx_place, [order.ready(x_near[0])] + x_near[1:], x_far, joint_back, (0, share), add=arrived
    )
    order.done(mine)
    in_totals = [middle(*in_parts[0][:2])]
    line_step(line_three, "down", 1)
    line_step(line_two, "up", 0)
    line_start("up", 1)
    wide_small = small_end(*wide_small)
    in_parts.append(begin(joint_rows[1], joint_matrices, True, 512))
    joint_all = from_all(mine)
    in_totals.append(middle(*in_parts[1][:2]))
    bias_sums = sum(p[3] for p in in_parts)
    late_small = small_start(
        jnp.concatenate([bias_sums[0, :columns], bias_sums[0, 2 * columns :]])
    )
    line_step(line_three, "up", 0)
    line_step(line_two, "up", 1)
    line_start("out", 0)
    late_small = small_step(*late_small)
    line_step(line_three, "up", 1)
    line_step(line_two, "out", 0)
    late_small = small_end(*late_small)
    line_step(line_three, "out", 0)

    input_low = []
    for r in each:
        near, far = in_totals[r]
        input_low.append(both((first[r] + (near.astype(F32) + far.astype(F32))).astype(BF16)))

    def whole_rows(values):
        stacked = jnp.stack([jnp.concatenate(pair, axis=0) for pair in values])
        return features_back(rotate(stacked, 1, core, 2))

    layer_output = whole_rows([both(v) for v in layer_low])
    input_grad = whole_rows(input_low).astype(F32)

    joint_grad = (
        joint_all.reshape(ctx, share, 3, HEAD).transpose(1, 2, 0, 3).reshape(share, 3, columns)
    ).astype(F32)

    wide = wide_small[: 6 * width].reshape(6, width)
    up_bias_grad = wide_small[6 * width :]
    qv_bias_grad = late_small.reshape(2, columns)

    def final(name, pieces, axis=0):
        return jnp.concatenate(
            [line_end(*lined[name, p]) for p in range(pieces)], axis=axis
        ).astype(F32)

    return (
        layer_output,
        input_grad,
        joint_grad,
        qv_bias_grad,
        final("out", 1),
        wide[3],
        wide[4],
        wide[5],
        final("up", 2, 1),
        up_bias_grad,
        final("down", 2),
        wide[0],
        wide[1],
        wide[2],
    )


def solution(mesh):
    weights = P("fsdp", None, "tp"), P(None, "tp"), P("tp", "fsdp")
    tokens = P("fsdp", "ctx", None)
    up, down = P("fsdp", "tp"), P("tp", "fsdp")
    tail = (P(), P(), P(), up, P("tp"), down, P(), P(), P())
    return jax.shard_map(
        local,
        mesh=mesh,
        in_specs=(tokens, P("fsdp", "ctx"), *weights, *tail, tokens),
        out_specs=(tokens, tokens, *weights, *tail),
        check_vma=False,
    )
```

```python
import functools
import math

import jax
import jax.numpy as jnp
from jax import lax
from jax.experimental import pallas as pl
from jax.experimental.pallas import tpu as pltpu
from jax.sharding import PartitionSpec as P

HEAD = 128
EPSILON = 1e-12
NEGATIVE = -1e30
LOG2E = 1.4426950408889634
SCALE = 1.0 / math.sqrt(HEAD)
VMEM_LIMIT = 56 * 2**20

BF16 = jnp.bfloat16
F32 = jnp.float32


def dot(left, right, left_dim, right_dim):
    return lax.dot_general(
        left, right, (((left_dim,), (right_dim,)), ((), ())), preferred_element_type=F32
    )


def params():
    return pltpu.CompilerParams(vmem_limit_bytes=VMEM_LIMIT)


def cost(flops, moved, special=0):
    return pl.CostEstimate(flops=flops // 256, bytes_accessed=moved // 256, transcendentals=0)


def like(shape, dtype):
    return jax.ShapeDtypeStruct(shape, dtype)


def core_swap(value):
    size = lax.axis_size("tp")
    return lax.ppermute(value, "tp", [(i, i ^ 1) for i in range(size)])


def chip_swap(value):
    size = lax.axis_size("tp")
    return lax.ppermute(value, "tp", [(i, i ^ 2) for i in range(size)])


def shift(value, axis, by):
    size = lax.axis_size(axis)
    return lax.ppermute(value, axis, [(i, (i + by) % size) for i in range(size)])


def rotate(value, axis, by, count):
    size = value.shape[axis]
    block = size // count
    if count == 1:
        return value
    twice = jnp.concatenate([value, value], axis=axis)
    if count == 2:
        swapped = lax.slice_in_dim(twice, block, block + size, axis=axis)
        return jnp.where(by == 0, value, swapped)
    return lax.dynamic_slice_in_dim(twice, by * block, size, axis=axis)


def after(value, *others):
    return lax.optimization_barrier((value, *others))[0]


class Order:
    def __init__(self):
        self.last = ()

    def ready(self, value):
        return after(value, *self.last) if self.last else value

    def done(self, value):
        self.last = (value,)
        return value

    def pin(self, value):
        self.last += (value,)


class Weight:
    def __init__(self, parts, axis, blocks, lead=None):
        self.parts, self.axis, self.blocks, self.lead = parts, axis, blocks, lead
        self.turned = len(parts) < blocks
        self.shape = list(parts[0].shape[-2:])
        if self.turned:
            self.shape[axis] //= blocks

    def arrays(self):
        return [self.parts[b % len(self.parts)] for b in range(self.blocks)]

    def specs(self, split_axis, tile):
        shape = list(self.shape)
        steps = shape[split_axis] // tile
        shape[split_axis] = tile

        def spec(block):
            def find(i, place_ref):
                at = [0, 0]
                if self.turned:
                    at[self.axis] = lax.rem(place_ref[0] + block, self.blocks)
                at[split_axis] = at[split_axis] * steps + i
                return tuple(at) if self.lead is None else (self.lead, *at)

            return pl.BlockSpec(tuple(shape) if self.lead is None else (None, *shape), find)

        return [spec(b) for b in range(self.blocks)]


def grid_call(kernel, name, place, grid, in_specs, out_specs, out_shape, scratch, estimate, values):
    return pl.pallas_call(
        kernel,
        grid_spec=pltpu.PrefetchScalarGridSpec(
            num_scalar_prefetch=1,
            grid=grid,
            in_specs=in_specs,
            out_specs=out_specs,
            scratch_shapes=scratch,
        ),
        out_shape=out_shape,
        compiler_params=params(),
        cost_estimate=estimate,
        name=name,
    )(place, *values)


def fixed(shape):
    return pl.BlockSpec(shape, lambda i, p: (0,) * len(shape))


def project_kernel(near, far, *refs):
    *weights, bias_ref, out = refs
    half = near.shape[0]
    depth = near.shape[1] // len(weights)
    for index, source in enumerate((near, far)):
        acc = bias_ref[...].astype(F32)
        for block, weight in enumerate(weights):
            acc = acc + dot(source[:, block * depth : (block + 1) * depth], weight[...], 1, 0)
        low = acc.astype(BF16)
        for kind in range(out.shape[0]):
            out[kind, index * half : (index + 1) * half, :] = low[:, kind * HEAD : (kind + 1) * HEAD]


def project(near, far, rows, weights, bias):
    tokens, width = near.shape
    half = tokens // rows
    columns = bias.shape[1]
    kinds = columns // HEAD
    token_spec = pl.BlockSpec((half, width), lambda i: (i, 0))
    whole = lambda i: (0, 0)
    return pl.pallas_call(
        project_kernel,
        grid=(rows,),
        in_specs=[token_spec] * 2
        + [pl.BlockSpec(w.shape, whole) for w in weights]
        + [pl.BlockSpec((1, columns), whole)],
        out_specs=pl.BlockSpec((kinds, 2 * half, HEAD), lambda i: (0, i, 0)),
        out_shape=like((kinds, 2 * tokens, HEAD), BF16),
        compiler_params=params(),
        cost_estimate=cost(4 * tokens * width * columns, 4 * (tokens * width + width * columns)),
        name="project",
    )(near, far, *weights, bias)


def up_kernel(blocks, place_ref, near, far, *refs):
    weights, bias_ref, act_ref, slope_ref = refs[:blocks], *refs[blocks:]
    half = near.shape[0]
    depth = near.shape[1] // blocks
    for index, source in enumerate((near, far)):
        pre = bias_ref[...].astype(F32)
        for block, weight in enumerate(weights):
            pre = pre + dot(source[:, block * depth : (block + 1) * depth], weight[...], 1, 0)
        square = pre * pre
        wave = jnp.tanh(pre * (0.7978845608028654 + 0.7978845608028654 * 0.044715 * square))
        half_up = 0.5 + 0.5 * wave
        slope = half_up + (0.5 * pre) * (1.0 - wave * wave) * (
            0.7978845608028654 + 3.0 * 0.7978845608028654 * 0.044715 * square
        )
        rows = slice(index * half, (index + 1) * half)
        act_ref[rows, :] = (pre * half_up).astype(BF16)
        slope_ref[rows, :] = slope.astype(slope_ref.dtype)


def up_project(place, near, far, weight, bias):
    half, width = near.shape
    columns = weight.shape[1]
    tile = 512
    out_spec = pl.BlockSpec((2 * half, tile), lambda i, p: (0, i))
    return grid_call(
        functools.partial(up_kernel, weight.blocks),
        "up_project",
        place,
        (columns // tile,),
        [fixed((half, width))] * 2
        + weight.specs(1, tile)
        + [pl.BlockSpec((1, tile), lambda i, p: (0, i))],
        [out_spec] * 2,
        [like((2 * half, columns), BF16)] * 2,
        [],
        cost(4 * half * width * columns, 2 * width * (2 * half + columns) + 8 * half * columns),
        [near, far, *weight.arrays(), bias],
    )


def act_back_kernel(blocks, place_ref, near, far, *refs):
    weights, slope_ref, out_ref, sum_ref = refs[:blocks], *refs[blocks:]
    half = near.shape[0]
    depth = near.shape[1] // blocks
    total = None
    for index, source in enumerate((near, far)):
        grad = None
        for block, weight in enumerate(weights):
            part = dot(source[:, block * depth : (block + 1) * depth], weight[...], 1, 1)
            grad = part if grad is None else grad + part
        rows = slice(index * half, (index + 1) * half)
        low = (grad * slope_ref[rows, :].astype(F32)).astype(BF16)
        out_ref[rows, :] = low
        part = jnp.sum(low.astype(F32), axis=0, keepdims=True)
        total = part if total is None else total + part
    sum_ref[...] = total


def act_back(place, near, far, weight, slope):
    half, width = near.shape
    columns = weight.shape[0]
    tile = 512
    out_spec = pl.BlockSpec((2 * half, tile), lambda i, p: (0, i))
    return grid_call(
        functools.partial(act_back_kernel, weight.blocks),
        "act_back",
        place,
        (columns // tile,),
        [fixed((half, width))] * 2 + weight.specs(0, tile) + [out_spec],
        [out_spec, pl.BlockSpec((1, tile), lambda i, p: (0, i))],
        [like((2 * half, columns), BF16), like((1, columns), F32)],
        [],
        cost(4 * half * width * columns, 2 * width * (2 * half + columns) + 8 * half * columns),
        [near, far, *weight.arrays(), slope],
    )


def head_back_kernel(blocks, place_ref, near, far, *refs):
    weights, out = refs[:blocks], refs[blocks]
    half = near.shape[0]
    depth = near.shape[1] // blocks
    for index, source in enumerate((near, far)):
        grad = None
        for block, weight in enumerate(weights):
            part = dot(source[:, block * depth : (block + 1) * depth], weight[...], 1, 1)
            grad = part if grad is None else grad + part
        low = grad.astype(BF16)
        for slot in range(out.shape[0]):
            out[slot, index * half : (index + 1) * half, :] = low[:, slot * HEAD : (slot + 1) * HEAD]


def head_back(place, near, far, weight):
    half, width = near.shape
    columns = weight.shape[0]
    heads = columns // HEAD
    return grid_call(
        functools.partial(head_back_kernel, weight.blocks),
        "head_back",
        place,
        (1,),
        [fixed((half, width))] * 2 + weight.specs(0, columns),
        fixed((heads, 2 * half, HEAD)),
        like((heads, 2 * half, HEAD), BF16),
        [],
        cost(4 * half * width * columns, 2 * width * (2 * half + columns)),
        [near, far, *weight.arrays()],
    )


def terms_kernel(transposed, blocks, parts, place_ref, left_ref, *refs):
    weights = refs[: blocks * parts]
    sent, kept, *rest = refs[blocks * parts :]
    at = pl.program_id(0)
    left = left_ref
    if rest:
        left = rest[0]

        @pl.when(at == 0)
        def _():
            if len(left_ref.shape) == 3:
                for head in range(left_ref.shape[0]):
                    left[:, head * HEAD : (head + 1) * HEAD] = left_ref[head]
            else:
                heads, kinds = left_ref.shape[:2]
                for head in range(heads):
                    for kind in range(kinds):
                        column = (kind * heads + head) * HEAD
                        left[:, column : column + HEAD] = left_ref[head, kind]
                rest[1][...] = jnp.sum(left[...].astype(F32), axis=0, keepdims=True)

    half = sent.shape[0]
    depth = left.shape[1] // parts
    share = sent.shape[1] // blocks
    for block in range(blocks):
        acc = None
        for part in range(parts):
            weight = weights[part * blocks + block]
            here = dot(
                left[:, part * depth : (part + 1) * depth], weight[...], 1, 1 if transposed else 0
            )
            acc = here if acc is None else acc + here
        tile = acc.shape[1]
        columns = pl.ds(pl.multiple_of(block * share + at * tile, tile), tile)
        kept[:, columns] = acc[:half]
        sent[:, columns] = acc[half:].astype(BF16)


def terms(place, left, weights, transposed, tile):
    tokens = left.shape[-2]
    blocks, parts = weights[0].blocks, len(weights)
    out_axis = 0 if transposed else 1
    share = weights[0].shape[out_axis]
    tile = min(tile, share)
    depth = math.prod(left.shape) // tokens
    half = tokens // 2
    outs = [like((half, blocks * share), BF16), like((half, blocks * share), F32)]
    if left.ndim > 2:
        outs.append(like((tokens, depth), BF16))
    if left.ndim > 3:
        outs.append(like((1, depth), F32))
    return grid_call(
        functools.partial(terms_kernel, transposed, blocks, parts),
        "terms",
        place,
        (share // tile,),
        [fixed(left.shape)] + [spec for w in weights for spec in w.specs(out_axis, tile)],
        [fixed(v.shape) for v in outs],
        outs,
        [],
        cost(
            2 * tokens * depth * blocks * share,
            2 * depth * (tokens + blocks * share) + 6 * half * blocks * share,
        ),
        [left] + [v for w in weights for v in w.arrays()],
    )


def grad_kernel(pairs, place_ref, *refs):
    out = refs[-1]
    acc = None
    for index in range(pairs):
        part = dot(refs[2 * index][...], refs[2 * index + 1][...], 0, 0)
        acc = part if acc is None else acc + part
    out[...] = acc.astype(out.dtype)


def weight_grad(pairs, rows, columns, place, blocks, split_left):
    row_from, row_count = rows
    col_from, col_count = columns
    row_tile = min(1024, row_count // blocks if split_left else row_count)
    col_tile = min(512, col_count if split_left else col_count // blocks)
    row_base, col_base = row_from // row_tile, col_from // col_tile
    specs, values, depth = [], [], 0
    row_per, col_per = row_count // blocks // row_tile, col_count // blocks // col_tile

    def turned(at, per, place_ref):
        return lax.rem(at // per + blocks - place_ref[0], blocks) * per + lax.rem(at, per)

    def left_map(first):
        if split_left:
            return lambda i, j, p: (first, turned(i, row_per, p))
        return lambda i, j, p: (first, i + row_base)

    def right_map(first):
        if split_left:
            return lambda i, j, p: (first, j + col_base)
        return lambda i, j, p: (first, turned(j, col_per, p))

    for (left, left_at), (right, right_at), height in pairs:
        specs.append(pl.BlockSpec((height, row_tile), left_map(left_at)))
        specs.append(pl.BlockSpec((height, col_tile), right_map(right_at)))
        values += [left, right]
        depth += height
    return pl.pallas_call(
        functools.partial(grad_kernel, len(pairs)),
        grid_spec=pltpu.PrefetchScalarGridSpec(
            num_scalar_prefetch=1,
            grid=(row_count // row_tile, col_count // col_tile),
            in_specs=specs,
            out_specs=pl.BlockSpec((row_tile, col_tile), lambda i, j, p: (i, j)),
        ),
        out_shape=like((row_count, col_count), BF16),
        compiler_params=params(),
        cost_estimate=cost(
            2 * row_count * col_count * depth,
            2 * (depth * row_count + depth * col_count + row_count * col_count),
        ),
        name="weight_grad",
    )(place, *values)


def joint_grad_kernel(rows, count, has_add, place_ref, *refs):
    heads, near, far = refs[:rows], refs[rows : rows + count], refs[rows + count : rows + 2 * count]
    out, scratch = refs[-2:]
    _, kinds, size, _ = heads[0].shape
    half = size // 2
    depth = rows * half

    @pl.when(pl.program_id(0) == 0)
    def _():
        for step in range(count):
            source = lax.rem(place_ref[0] + count - step, count)
            for row, head in enumerate(heads):
                for part in range(2):
                    start = ((step * 2 + part) * rows + row) * half
                    for kind in range(kinds):
                        scratch[start : start + half, kind * HEAD : (kind + 1) * HEAD] = head[
                            source, kind, part * half : (part + 1) * half, :
                        ]

    acc = None
    for index in range(2 * count):
        left = (near, far)[index % 2][index // 2]
        part = dot(left[...], scratch[index * depth : (index + 1) * depth, :], 0, 0)
        acc = part if acc is None else acc + part
    if has_add:
        acc = acc + refs[rows + 2 * count][...].astype(F32)
    out[...] = acc.astype(BF16)


def joint_grad_terms(place, near, far, heads, left_cols, add=None):
    row_from, rows = left_cols
    tile = min(256, rows)
    base = row_from // tile
    places, kinds, size, _ = heads[0].shape
    depth = near[0].shape[0]
    specs = [pl.BlockSpec(h.shape, lambda i, p: (0, 0, 0, 0)) for h in heads]
    specs += [pl.BlockSpec((depth, tile), lambda i, p: (0, i + base))] * (2 * places)
    values = [*heads, *near, *far]
    if add is not None:
        specs.append(pl.BlockSpec((tile, kinds * HEAD), lambda i, p: (i, 0)))
        values.append(add)
    return pl.pallas_call(
        functools.partial(joint_grad_kernel, len(heads), places, add is not None),
        grid_spec=pltpu.PrefetchScalarGridSpec(
            num_scalar_prefetch=1,
            grid=(rows // tile,),
            in_specs=specs,
            out_specs=pl.BlockSpec((tile, kinds * HEAD), lambda i, p: (i, 0)),
            scratch_shapes=[pltpu.VMEM((2 * places * depth, kinds * HEAD), BF16)],
        ),
        out_shape=like((rows, kinds * HEAD), BF16),
        compiler_params=params(),
        cost_estimate=cost(
            4 * places * depth * rows * kinds * HEAD, 4 * places * depth * (rows + kinds * HEAD)
        ),
        name="joint_grad",
    )(place, *values)


def gather_blocks(scratch, source):
    count, size, _ = source.shape
    for index in range(count):
        scratch[index * size : (index + 1) * size, :] = source[index]


def gather_kinds(place_ref, sources, scratches, turned=None):
    count = len(sources)
    for step, source in enumerate(sources):
        size = source.shape[1]
        start = lax.rem(place_ref[0] + count - step, count) * size
        rows = pl.ds(pl.multiple_of(start, size), size)
        for kind, scratch in enumerate(scratches):
            scratch[rows, :] = source[kind]
        if turned is not None:
            turned[:, rows] = source[1].T


def put_rows(out, at, query_block, value, lead=()):
    size = out.shape[-2]
    per = query_block // size
    for slot in range(per):
        out[(at * per + slot, *lead)] = value[slot * size : (slot + 1) * size]


def attend_kernel(parts, query_block, key_block, live, place_ref, *refs):
    seg_row, seg_col, out, mixed_ref, total_ref = refs[parts : parts + 5]
    qs, ks, vs, scores, top, total, mixed = refs[parts + 5 :]
    at = pl.program_id(0)
    count = qs.shape[0] // key_block

    @pl.when(at == 0)
    def _():
        gather_kinds(place_ref, refs[:parts], (qs, ks, vs))

    here = pl.ds(pl.multiple_of(at * query_block, query_block), query_block)
    query = qs[here, :]
    seg_query = seg_row[:, here]
    top[...] = jnp.full_like(top, NEGATIVE)
    total[...] = jnp.zeros_like(total)
    mixed[...] = jnp.zeros_like(mixed)

    def score(step, masked):
        rows = pl.ds(pl.multiple_of(step * key_block, key_block), key_block)
        raw = dot(ks[rows, :], query, 1, 1) * (LOG2E * SCALE)
        if masked:
            raw = jnp.where(seg_col[rows, 0:1] == seg_query, raw, NEGATIVE)
        scores[rows, :] = raw
        top[...] = jnp.maximum(top[...], jnp.max(raw, axis=0, keepdims=True))

    def first(step, carry):
        pl.when(live[at, step] == 1)(functools.partial(score, step, True))
        pl.when(live[at, step] == 2)(functools.partial(score, step, False))
        return carry

    def second(step, carry):
        @pl.when(live[at, step] > 0)
        def _():
            rows = pl.ds(pl.multiple_of(step * key_block, key_block), key_block)
            weight = jnp.exp2(scores[rows, :] - top[...])
            total[...] += jnp.sum(weight, axis=0, keepdims=True)
            mixed[...] += dot(vs[rows, :], weight.astype(BF16), 0, 0)

        return carry

    lax.fori_loop(0, count, first, 0)
    lax.fori_loop(0, count, second, 0)
    result = mixed[...] / total[...]
    mixed_ref[:, here] = result
    total_ref[:, here] = top[...] + jnp.log2(total[...])
    put_rows(out, at, query_block, result.T.astype(BF16))


def attend(row, place, heads, seg_row, seg_col, live):
    parts = len(heads)
    length = seg_row.shape[2]
    size = length // parts
    query_block, key_block = length // live.shape[1], length // live.shape[2]
    part_spec = pl.BlockSpec((3, size, HEAD), lambda i, s, p: (0, row, 0))
    whole = lambda i, s, p: (0, 0)
    return pl.pallas_call(
        functools.partial(attend_kernel, parts, query_block, key_block),
        grid_spec=pltpu.PrefetchScalarGridSpec(
            num_scalar_prefetch=2,
            grid=(length // query_block,),
            in_specs=[part_spec] * parts
            + [
                pl.BlockSpec((None, 1, length), lambda i, s, p: (row, 0, 0)),
                pl.BlockSpec((None, length, HEAD), lambda i, s, p: (row, 0, 0)),
            ],
            out_specs=[
                pl.BlockSpec((parts, size, HEAD), lambda i, s, p: (0, 0, 0)),
                pl.BlockSpec((HEAD, length), whole),
                pl.BlockSpec((1, length), whole),
            ],
            scratch_shapes=[pltpu.VMEM((length, HEAD), BF16)] * 3
            + [
                pltpu.VMEM((length, query_block), F32),
                pltpu.VMEM((1, query_block), F32),
                pltpu.VMEM((1, query_block), F32),
                pltpu.VMEM((HEAD, query_block), F32),
            ],
        ),
        out_shape=[
            like((parts, size, HEAD), BF16),
            like((HEAD, length), F32),
            like((1, length), F32),
        ],
        compiler_params=params(),
        cost_estimate=cost(4 * length * length * HEAD, 8 * length * HEAD, length * length // 2),
        name="attend",
    )(live[row], place, *heads, seg_row, seg_col)


def attend_back_kernel(parts, query_block, key_block, live, place_ref, *refs):
    g_in, seg_row, seg_col, mixed_ref, total_ref, out = refs[parts : parts + 6]
    qs, ks, vs, gs, kt, d_keys, d_values, d_query = refs[parts + 6 :]
    at = pl.program_id(0)
    count = qs.shape[0] // key_block

    @pl.when(at == 0)
    def _():
        gather_kinds(place_ref, refs[:parts], (qs, ks, vs), kt)
        gather_blocks(gs, g_in)
        d_keys[...] = jnp.zeros_like(d_keys)
        d_values[...] = jnp.zeros_like(d_values)

    here = pl.ds(pl.multiple_of(at * query_block, query_block), query_block)
    query = qs[here, :]
    grad = gs[here, :]
    seg_query = seg_row[:, here]
    log_total = total_ref[:, here]
    weighted = jnp.sum(mixed_ref[:, here] * grad.astype(F32).T, axis=0, keepdims=True)
    d_query[...] = jnp.zeros_like(d_query)

    def back(step, masked):
        rows = pl.ds(pl.multiple_of(step * key_block, key_block), key_block)
        key, value = ks[rows, :], vs[rows, :]
        raw = dot(key, query, 1, 1) * (LOG2E * SCALE)
        if masked:
            raw = jnp.where(seg_col[rows, 0:1] == seg_query, raw, NEGATIVE)
        probs = jnp.exp2(raw - log_total)
        d_scores = (probs * (dot(value, grad, 1, 1) - weighted)).astype(BF16)
        d_values[rows, :] += dot(probs.astype(BF16), grad, 1, 0)
        d_keys[rows, :] += dot(d_scores, query, 1, 0)
        d_query[...] += dot(kt[:, rows], d_scores, 1, 0)

    def step_of(step, carry):
        pl.when(live[at, step] == 1)(functools.partial(back, step, True))
        pl.when(live[at, step] == 2)(functools.partial(back, step, False))
        return carry

    lax.fori_loop(0, count, step_of, 0)
    put_rows(out, at, query_block, (d_query[...] * SCALE).T.astype(BF16), (0,))

    @pl.when(at == pl.num_programs(0) - 1)
    def _():
        size = out.shape[2]
        for slot in range(out.shape[0]):
            rows = slice(slot * size, (slot + 1) * size)
            out[slot, 1] = (d_keys[rows, :] * SCALE).astype(BF16)
            out[slot, 2] = d_values[rows, :].astype(BF16)


def attend_back(row, place, heads, grads, seg_row, seg_col, live, mixed, totals):
    parts = len(heads)
    length = seg_row.shape[2]
    size = length // parts
    query_block, key_block = length // live.shape[1], length // live.shape[2]
    part_spec = pl.BlockSpec((3, size, HEAD), lambda i, s, p: (0, row, 0))
    whole = lambda i, s, p: (0, 0)
    return pl.pallas_call(
        functools.partial(attend_back_kernel, parts, query_block, key_block),
        grid_spec=pltpu.PrefetchScalarGridSpec(
            num_scalar_prefetch=2,
            grid=(length // query_block,),
            in_specs=[part_spec] * parts
            + [
                pl.BlockSpec((parts, size, HEAD), lambda i, s, p: (0, 0, 0)),
                pl.BlockSpec((None, 1, length), lambda i, s, p: (row, 0, 0)),
                pl.BlockSpec((None, length, HEAD), lambda i, s, p: (row, 0, 0)),
                pl.BlockSpec((HEAD, length), whole),
                pl.BlockSpec((1, length), whole),
            ],
            out_specs=pl.BlockSpec((parts, 3, size, HEAD), lambda i, s, p: (0, 0, 0, 0)),
            scratch_shapes=[pltpu.VMEM((length, HEAD), BF16)] * 4
            + [pltpu.VMEM((HEAD, length), BF16)]
            + [pltpu.VMEM((length, HEAD), F32)] * 2
            + [pltpu.VMEM((HEAD, query_block), F32)],
        ),
        out_shape=like((parts, 3, size, HEAD), BF16),
        compiler_params=params(),
        cost_estimate=cost(10 * length * length * HEAD, 16 * length * HEAD, length * length // 2),
        name="attend_back",
    )(live[row], place, *heads, grads, seg_row, seg_col, mixed, totals)


def normalize(hidden):
    center = hidden - jnp.mean(hidden, axis=-1, keepdims=True)
    inverse = lax.rsqrt(jnp.mean(center * center, axis=-1, keepdims=True) + EPSILON)
    return center * inverse, inverse


def normalize_back(grad, normal, inverse):
    return inverse * (
        grad
        - jnp.mean(grad, axis=-1, keepdims=True)
        - normal * jnp.mean(grad * normal, axis=-1, keepdims=True)
    )


def add_up(ref, values):
    @pl.when(pl.program_id(0) == 0)
    def _():
        ref[...] = jnp.zeros_like(ref)

    ref[...] += jnp.concatenate([jnp.sum(v, axis=0, keepdims=True) for v in values], axis=0)


def norm_one_kernel(near, far, x, vectors, normal_ref, inverse_ref, low_ref):
    hidden = x[...].astype(F32) + (near[...].astype(F32) + far[...].astype(F32)) + vectors[0:1, :]
    normal, inverse = normalize(hidden)
    normal_ref[...] = normal
    inverse_ref[...] = jnp.broadcast_to(inverse, inverse_ref.shape)
    low_ref[...] = (normal * vectors[1:2, :] + vectors[2:3, :]).astype(BF16)


def norm_two_kernel(near, far, normal_one, grad_ref, vectors, out_ref, second_ref, low_ref, sum_ref):
    hidden = (
        normal_one[...] * vectors[1:2, :]
        + vectors[2:3, :]
        + (near[...].astype(F32) + far[...].astype(F32))
        + vectors[3:4, :]
    )
    normal, inverse = normalize(hidden)
    out_ref[...] = (normal * vectors[4:5, :] + vectors[5:6, :]).astype(BF16)
    grad = grad_ref[...].astype(F32)
    d_hidden = normalize_back(grad * vectors[4:5, :], normal, inverse)
    low = d_hidden.astype(BF16)
    second_ref[...] = d_hidden
    low_ref[...] = low
    add_up(sum_ref, (low.astype(F32), grad * normal, grad))


def norm_back_kernel(near, far, second, normal_ref, inverse_ref, vectors, first_ref, low_ref, sum_ref):
    d_norm = second[...] + (near[...].astype(F32) + far[...].astype(F32))
    normal = normal_ref[...]
    d_hidden = normalize_back(d_norm * vectors[1:2, :], normal, inverse_ref[:, 0:1])
    low = d_hidden.astype(BF16)
    first_ref[...] = d_hidden
    low_ref[...] = low
    add_up(sum_ref, (low.astype(F32), d_norm * normal, d_norm))


def by_tokens(kernel, name, inputs, vectors, outs, sums=0):
    tokens, width = inputs[0][0].shape
    tile = tokens // 4
    specs = [
        pl.BlockSpec((tile, v.shape[1]), lambda i, a=at: (a * 4 + i, 0)) for v, at in inputs
    ]
    out_specs = [pl.BlockSpec((tile, columns), lambda i: (i, 0)) for columns, _ in outs]
    out_shape = [like((tokens, columns), dtype) for columns, dtype in outs]
    if sums:
        out_specs.append(pl.BlockSpec((sums, width), lambda i: (0, 0)))
        out_shape.append(like((sums, width), F32))
    return pl.pallas_call(
        kernel,
        grid=(4,),
        in_specs=specs + [pl.BlockSpec(vectors.shape, lambda i: (0, 0))],
        out_specs=out_specs,
        out_shape=out_shape,
        compiler_params=params(),
        cost_estimate=cost(20 * tokens * width, 16 * tokens * width),
        name=name,
    )(*[v for v, _ in inputs], vectors)


def local(
    layer_input,
    segment_ids,
    qkv_weight,
    qv_bias,
    out_weight,
    out_bias,
    norm1_gain,
    norm1_bias,
    up_weight,
    up_bias,
    down_weight,
    down_bias,
    norm2_gain,
    norm2_bias,
    out_grad,
):
    rows, local_len, width = layer_input.shape
    fsdp, ctx = lax.axis_size("fsdp"), lax.axis_size("ctx")
    y, place = lax.axis_index("fsdp"), lax.axis_index("ctx")
    core, chip = lax.axis_index("tp") % 2, lax.axis_index("tp") // 2
    columns = qkv_weight.shape[2]
    hidden_units = up_weight.shape[1]
    heads = columns // HEAD
    half = local_len // 2
    share = width // fsdp
    each = range(rows)
    assert heads == ctx == 4 and lax.axis_size("tp") == 4
    order = Order()

    def features(value):
        return rotate(value, value.ndim - 1, y, fsdp)

    def features_back(value):
        return rotate(value, value.ndim - 1, (fsdp - y) % fsdp, fsdp)

    def spread(block):
        return [block] + [shift(block, "fsdp", -by) for by in range(1, fsdp)]

    def swap_ctx(value):
        return lax.all_to_all(value, "ctx", 0, 0, tiled=True)

    def from_all(value):
        return swap_ctx(jnp.broadcast_to(value[None], (ctx, *value.shape)))

    def both(value):
        return value, core_swap(value)

    seg_own = rotate(segment_ids, 1, core, 2)
    seg = from_all(seg_own).transpose(1, 0, 2).reshape(rows, ctx * local_len)

    first_token = core * half + chip * (half // 2)
    quarter = features(lax.dynamic_slice_in_dim(layer_input, first_token, half // 2, axis=1))
    x_rows = features(rotate(layer_input, 1, core, 2))
    x = x_rows.reshape(rows * local_len, width)

    vectors = features(
        jnp.stack([out_bias, norm1_gain, norm1_bias, down_bias, norm2_gain, norm2_bias])
    ).astype(F32)
    grad_half = features(
        lax.dynamic_slice_in_dim(out_grad, core * half, half, axis=1)
    ).reshape(rows * half, width)

    fsdp_place = y.astype(jnp.int32)[None]
    ctx_place = place.astype(jnp.int32)[None]

    mine = lax.dynamic_slice_in_dim(qkv_weight, place * HEAD, HEAD, axis=2)
    head_weight = spread(mine.reshape(share, 3 * HEAD))
    bias_pair = lax.dynamic_slice_in_dim(qv_bias, place * HEAD, HEAD, axis=1)
    head_bias = jnp.concatenate(
        [bias_pair[:1], jnp.zeros_like(bias_pair[:1]), bias_pair[1:]], axis=1
    )

    def joined(quarter, other):
        parts = jnp.stack([quarter, other], axis=1).reshape(rows, half, width)
        return rotate(parts, 1, chip, 2).reshape(rows * half, width)

    def flat(value):
        return value.reshape(rows * half, width)

    x_near, x_far = [flat(x_rows[:, :half])], [flat(x_rows[:, half:])]
    quarter, seg = lax.optimization_barrier((quarter, seg))
    first_quarter = shift(quarter, "ctx", 1)
    heads_all = [project(x_near[0], x_far[0], rows, head_weight, head_bias)]
    second_quarter = shift(first_quarter, "ctx", 1)
    x_near.append(joined(first_quarter, chip_swap(first_quarter)))
    x_far.append(core_swap(x_near[1]))
    third_quarter = shift(after(second_quarter, x_near[1]), "ctx", 1)
    heads_all.append(project(x_near[1], x_far[1], rows, head_weight, head_bias))
    x_near.append(joined(second_quarter, chip_swap(second_quarter)))
    x_far.append(core_swap(x_near[2]))
    heads_all.append(project(x_near[2], x_far[2], rows, head_weight, head_bias))
    third_other = chip_swap(after(third_quarter, heads_all[0], x_near[2]))
    third_quarter = after(third_quarter, heads_all[1], heads_all[2])
    x_near.append(joined(third_quarter, third_other))
    x_far.append(core_swap(x_near[3]))
    heads_all.append(order.done(project(x_near[3], x_far[3], rows, head_weight, head_bias)))

    gate = [*head_weight[1:], first_quarter]

    def whole(block, axis):
        return lax.all_gather(after(block, *gate), "fsdp", axis=axis, tiled=True)

    out_full = Weight([whole(out_weight, 1)], 1, fsdp)
    up_full = Weight([whole(up_weight, 0)], 0, fsdp)
    down_full = Weight([whole(down_weight, 1)], 1, fsdp)
    joint_full = whole(jnp.stack([qkv_weight[:, j] for j in range(3)]), 1)
    joint_matrices = [Weight([joint_full], 0, fsdp, j) for j in range(3)]

    length = ctx * local_len
    seg_row = seg[:, None, :]
    seg_col = jnp.broadcast_to(seg[:, :, None], (rows, length, HEAD))

    def span(size):
        blocks = seg.reshape(rows, length // size, size)
        return jnp.min(blocks, axis=2), jnp.max(blocks, axis=2)

    (query_low, query_high), (key_low, key_high) = span(2 * local_len), span(local_len)
    meets = (query_low[:, :, None] <= key_high[:, None, :]) & (
        key_low[:, None, :] <= query_high[:, :, None]
    )
    same = (query_low == query_high)[:, :, None] & (key_low == key_high)[:, None, :] & meets
    live = meets.astype(jnp.int32) + same.astype(jnp.int32)

    attended, kept = [], []
    for r in each:
        pieces, mixed, totals = attend(
            r, ctx_place, [order.ready(heads_all[0]), *heads_all[1:]], seg_row, seg_col, live
        )
        order.done(totals)
        kept.append((mixed, totals))
        attended.append(swap_ctx(pieces))

    def begin(left, weights, transposed, tile):
        sent, mine, *rest = terms(order.ready(fsdp_place), left, weights, transposed, tile)
        order.done(sent)
        return core_swap(sent), mine, *rest

    def middle(near, mine):
        total = order.done((order.ready(mine) + near.astype(F32)).astype(BF16))
        return total, chip_swap(total)

    parts = [begin(attended[r], [out_full], False, 512) for r in each]
    attended_last = attended[-1]
    attended = [parts[r][2] for r in each]
    totals = [middle(*parts[r][:2]) for r in each]

    normal_one, inverse_one, norm_low = [], [], []
    for r in each:
        near, far = totals[r]
        normal, inverse, low = by_tokens(
            norm_one_kernel,
            "norm_one",
            [(order.ready(near), 0), (far, 0), (x, 2 * r)],
            vectors,
            [(width, F32), (HEAD, F32), (width, BF16)],
        )
        order.done(low)
        normal_one.append(normal)
        inverse_one.append(inverse)
        norm_low.append(both(low))

    act_low, slopes = [], []
    for r in each:
        near, far = norm_low[r]
        act, slope = up_project(fsdp_place, order.ready(near), far, up_full, up_bias[None])
        order.done(act)
        act_low.append(act)
        slopes.append(slope)

    parts = [begin(act_low[r], [down_full], False, 512) for r in each]
    totals = [middle(*parts[r]) for r in each]

    layer_low, second, mlp_low, sums_two = [], [], [], []
    pre_low, up_sums, up_parts = [], [], []

    def norm_two(r):
        near, far = totals[r]
        out, d_second, low, sums = by_tokens(
            norm_two_kernel,
            "norm_two",
            [(order.ready(near), 0), (far, 0), (normal_one[r], 0), (grad_half, r)],
            vectors,
            [(width, BF16), (width, F32), (width, BF16)],
            3,
        )
        order.done(low)
        layer_low.append(out)
        second.append(d_second)
        mlp_low.append(both(low))
        sums_two.append(sums)

    def act_step(r):
        near, far = mlp_low[r]
        low, sums = act_back(fsdp_place, order.ready(near), far, down_full, slopes[r])
        order.done(low)
        pre_low.append(low)
        up_sums.append(sums)

    def up_step(r):
        up_parts.append(begin(pre_low[r], [up_full], True, 512))

    halves = range(2)
    gradients = {}

    def pairs_of(left, right):
        made = []
        for r in each:
            for h in halves:
                a = (left[r][h], 0) if isinstance(left[r], tuple) else (left[r], h)
                b = (right[r][h], 0) if isinstance(right[r], tuple) else (right[r], h)
                made.append((a, b, half))
        return made

    def give(name, pairs, shape, split_left, piece, pieces):
        (left, *others) = pairs
        left = ((order.ready(left[0][0]), left[0][1]), *left[1:])
        if split_left:
            part = shape[1] // pieces
            ranges = (0, shape[0]), (piece * part, part)
        else:
            part = shape[0] // pieces
            ranges = (piece * part, part), (0, shape[1])
        mine = order.done(
            weight_grad([left, *others], *ranges, fsdp_place, fsdp, split_left)
        )
        gradients[name, piece] = lax.psum_scatter(
            mine, "fsdp", scatter_dimension=0 if split_left else 1, tiled=True
        )

    def line_one(value):
        return value, lax.ppermute(value, "ctx", [(0, 1), (3, 2)])

    def line_two(value, other):
        pair = order.done((order.ready(value).astype(F32) + other.astype(F32)).astype(BF16))
        return pair, lax.ppermute(pair, "ctx", [(1, 2), (2, 1)])

    def line_three(pair, other):
        total = order.done((order.ready(pair).astype(F32) + other.astype(F32)).astype(BF16))
        return total, lax.ppermute(total, "ctx", [(1, 0), (2, 3)])

    outer = (place == 0) | (place == ctx - 1)

    def line_end(total, other):
        return jnp.where(outer, other, total)

    first, attn_low, sums_one, head_grads = [], [], [], []

    def norm_back(r):
        near, far = up_totals[r]
        d_first, low, sums = by_tokens(
            norm_back_kernel,
            "norm_back",
            [(order.ready(near), 0), (far, 0), (second[r], 0), (normal_one[r], 0), (inverse_one[r], 0)],
            vectors,
            [(width, F32), (width, BF16)],
            3,
        )
        order.done(low)
        first.append(d_first)
        attn_low.append(both(low))
        sums_one.append(sums)

    def head_step(r):
        near, far = attn_low[r]
        pieces = order.done(head_back(fsdp_place, order.ready(near), far, out_full))
        head_grads.append(swap_ctx(pieces))

    joint_back, joint_rows = [], []

    def attend_step(r):
        mixed, row_totals = kept[r]
        place_now = order.ready(ctx_place)
        pieces = attend_back(
            r, place_now, heads_all, head_grads[r], seg_row, seg_col, live, mixed, row_totals
        )
        joint_back.append(order.done(pieces))
        joint_rows.append(swap_ctx(pieces))

    lined = {}

    def line_start(name, piece):
        lined[name, piece] = line_one(gradients[name, piece])

    def line_step(step, name, piece):
        lined[name, piece] = step(*lined[name, piece])

    def small_start(value):
        value = value + shift(value, "fsdp", 1) if fsdp == 2 else lax.psum(value, "fsdp")
        return value, lax.ppermute(value, "ctx", [(0, 1), (1, 0), (2, 3), (3, 2)])

    def small_step(value, other):
        value = order.done(order.ready(value) + other)
        return value, lax.ppermute(value, "ctx", [(0, 2), (2, 0), (1, 3), (3, 1)])

    def small_end(value, other):
        return order.done(order.ready(value) + other)

    norm_two(0)
    act_step(0)
    up_step(0)
    order.pin(joint_full)
    norm_two(1)
    up_totals = [middle(*up_parts[0])]
    down_args = (pairs_of(act_low, mlp_low), (hidden_units, width), False)
    give("down", *down_args, 0, 2)
    act_step(1)
    up_step(1)
    give("down", *down_args, 1, 2)
    up_totals.append(middle(*up_parts[1]))
    up_args = (pairs_of(norm_low, pre_low), (width, hidden_units), True)
    norm_back(0)
    give("up", *up_args, 0, 2)
    order.pin(gradients["down", 0])
    head_step(0)
    line_start("down", 0)
    order.pin(head_grads[0])
    line_step(line_two, "down", 0)
    norm_back(1)
    order.pin(gradients["down", 1])
    give("up", *up_args, 1, 2)
    line_start("down", 1)
    head_step(1)
    out_args = (pairs_of(attended, attn_low), (columns, width), False)
    give("out", *out_args, 0, 1)
    wide = features_back(jnp.concatenate([sum(sums_two), sum(sums_one)], axis=0))
    wide = wide + core_swap(wide)
    attend_step(0)
    wide_small = small_start(jnp.concatenate([wide.reshape(-1), sum(up_sums).reshape(-1)]))
    order.pin(gradients["up", 0])
    line_step(line_three, "down", 0)
    line_step(line_two, "down", 1)
    line_start("up", 0)
    attend_step(1)

    arrived = None
    for by in range(1, fsdp):
        sent = joint_grad_terms(
            ctx_place, [order.ready(x_near[0])] + x_near[1:], x_far, joint_back, (by * share, share)
        )
        got = shift(order.done(sent), "fsdp", by)
        arrived = got if arrived is None else (arrived.astype(F32) + got.astype(F32))

    order.pin(gradients["up", 1])
    line_step(line_three, "down", 1)
    line_step(line_two, "up", 0)
    line_start("up", 1)
    wide_small = small_step(*wide_small)
    order.pin(arrived)
    in_parts = [begin(joint_rows[0], joint_matrices, True, 512)]
    mine = joint_grad_terms(
        ctx_place, [order.ready(x_near[0])] + x_near[1:], x_far, joint_back, (0, share), add=arrived
    )
    order.done(mine)
    in_totals = [middle(*in_parts[0][:2])]
    order.pin(gradients["out", 0])
    line_step(line_three, "up", 0)
    line_step(line_two, "up", 1)
    line_start("out", 0)
    wide_small = small_end(*wide_small)
    in_parts.append(begin(joint_rows[1], joint_matrices, True, 512))
    joint_all = from_all(mine)
    in_totals.append(middle(*in_parts[1][:2]))
    bias_sums = sum(p[3] for p in in_parts)
    late_small = small_start(
        jnp.concatenate([bias_sums[0, :columns], bias_sums[0, 2 * columns :]])
    )
    line_step(line_three, "up", 1)
    line_step(line_two, "out", 0)
    late_small = small_step(*late_small)
    line_step(line_three, "out", 0)
    late_small = small_end(*late_small)

    input_low = []
    for r in each:
        near, far = in_totals[r]
        input_low.append(both((first[r] + (near.astype(F32) + far.astype(F32))).astype(BF16)))

    def whole_rows(values):
        stacked = jnp.stack([jnp.concatenate(pair, axis=0) for pair in values])
        return features_back(rotate(stacked, 1, core, 2))

    layer_output = whole_rows([both(v) for v in layer_low])
    input_grad = whole_rows(input_low).astype(F32)

    joint_grad = (
        joint_all.reshape(ctx, share, 3, HEAD).transpose(1, 2, 0, 3).reshape(share, 3, columns)
    ).astype(F32)

    wide = wide_small[: 6 * width].reshape(6, width)
    up_bias_grad = wide_small[6 * width :]
    qv_bias_grad = late_small.reshape(2, columns)

    def final(name, pieces, axis=0):
        return jnp.concatenate(
            [line_end(*lined[name, p]) for p in range(pieces)], axis=axis
        ).astype(F32)

    return (
        layer_output,
        input_grad,
        joint_grad,
        qv_bias_grad,
        final("out", 1),
        wide[3],
        wide[4],
        wide[5],
        final("up", 2, 1),
        up_bias_grad,
        final("down", 2),
        wide[0],
        wide[1],
        wide[2],
    )


def solution(mesh):
    weights = P("fsdp", None, "tp"), P(None, "tp"), P("tp", "fsdp")
    tokens = P("fsdp", "ctx", None)
    up, down = P("fsdp", "tp"), P("tp", "fsdp")
    tail = (P(), P(), P(), up, P("tp"), down, P(), P(), P())
    return jax.shard_map(
        local,
        mesh=mesh,
        in_specs=(tokens, P("fsdp", "ctx"), *weights, *tail, tokens),
        out_specs=(tokens, tokens, *weights, *tail),
        check_vma=False,
    )
```

```python
import functools
import math

import jax
import jax.numpy as jnp
from jax import lax
from jax.experimental import pallas as pl
from jax.experimental.pallas import tpu as pltpu
from jax.sharding import PartitionSpec as P

HEAD = 128
EPSILON = 1e-12
NEGATIVE = -1e30
LOG2E = 1.4426950408889634
SCALE = 1.0 / math.sqrt(HEAD)
VMEM_LIMIT = 56 * 2**20

BF16 = jnp.bfloat16
F32 = jnp.float32


def dot(left, right, left_dim, right_dim):
    return lax.dot_general(
        left, right, (((left_dim,), (right_dim,)), ((), ())), preferred_element_type=F32
    )


def params():
    return pltpu.CompilerParams(vmem_limit_bytes=VMEM_LIMIT)


def cost(flops, moved, special=0):
    return pl.CostEstimate(flops=flops // 256, bytes_accessed=moved // 256, transcendentals=0)


def like(shape, dtype):
    return jax.ShapeDtypeStruct(shape, dtype)


def core_swap(value):
    size = lax.axis_size("tp")
    return lax.ppermute(value, "tp", [(i, i ^ 1) for i in range(size)])


def chip_swap(value):
    size = lax.axis_size("tp")
    return lax.ppermute(value, "tp", [(i, i ^ 2) for i in range(size)])


def shift(value, axis, by):
    size = lax.axis_size(axis)
    return lax.ppermute(value, axis, [(i, (i + by) % size) for i in range(size)])


def rotate(value, axis, by, count):
    size = value.shape[axis]
    block = size // count
    if count == 1:
        return value
    twice = jnp.concatenate([value, value], axis=axis)
    if count == 2:
        swapped = lax.slice_in_dim(twice, block, block + size, axis=axis)
        return jnp.where(by == 0, value, swapped)
    return lax.dynamic_slice_in_dim(twice, by * block, size, axis=axis)


def after(value, *others):
    return lax.optimization_barrier((value, *others))[0]


class Order:
    def __init__(self):
        self.last = ()

    def ready(self, value):
        return after(value, *self.last) if self.last else value

    def done(self, value):
        self.last = (value,)
        return value

    def pin(self, value):
        self.last += (value,)


class Weight:
    def __init__(self, parts, axis, blocks, lead=None):
        self.parts, self.axis, self.blocks, self.lead = parts, axis, blocks, lead
        self.turned = len(parts) < blocks
        self.shape = list(parts[0].shape[-2:])
        if self.turned:
            self.shape[axis] //= blocks

    def arrays(self):
        return [self.parts[b % len(self.parts)] for b in range(self.blocks)]

    def specs(self, split_axis, tile):
        shape = list(self.shape)
        steps = shape[split_axis] // tile
        shape[split_axis] = tile

        def spec(block):
            def find(i, place_ref):
                at = [0, 0]
                if self.turned:
                    at[self.axis] = lax.rem(place_ref[0] + block, self.blocks)
                at[split_axis] = at[split_axis] * steps + i
                return tuple(at) if self.lead is None else (self.lead, *at)

            return pl.BlockSpec(tuple(shape) if self.lead is None else (None, *shape), find)

        return [spec(b) for b in range(self.blocks)]


def grid_call(kernel, name, place, grid, in_specs, out_specs, out_shape, scratch, estimate, values):
    return pl.pallas_call(
        kernel,
        grid_spec=pltpu.PrefetchScalarGridSpec(
            num_scalar_prefetch=1,
            grid=grid,
            in_specs=in_specs,
            out_specs=out_specs,
            scratch_shapes=scratch,
        ),
        out_shape=out_shape,
        compiler_params=params(),
        cost_estimate=estimate,
        name=name,
    )(place, *values)


def fixed(shape):
    return pl.BlockSpec(shape, lambda i, p: (0,) * len(shape))


def project_kernel(near, far, *refs):
    *weights, bias_ref, out = refs
    half = near.shape[0]
    depth = near.shape[1] // len(weights)
    for index, source in enumerate((near, far)):
        acc = bias_ref[...].astype(F32)
        for block, weight in enumerate(weights):
            acc = acc + dot(source[:, block * depth : (block + 1) * depth], weight[...], 1, 0)
        low = acc.astype(BF16)
        for kind in range(out.shape[0]):
            out[kind, index * half : (index + 1) * half, :] = low[:, kind * HEAD : (kind + 1) * HEAD]


def project(near, far, rows, weights, bias):
    tokens, width = near.shape
    half = tokens // rows
    columns = bias.shape[1]
    kinds = columns // HEAD
    token_spec = pl.BlockSpec((half, width), lambda i: (i, 0))
    whole = lambda i: (0, 0)
    return pl.pallas_call(
        project_kernel,
        grid=(rows,),
        in_specs=[token_spec] * 2
        + [pl.BlockSpec(w.shape, whole) for w in weights]
        + [pl.BlockSpec((1, columns), whole)],
        out_specs=pl.BlockSpec((kinds, 2 * half, HEAD), lambda i: (0, i, 0)),
        out_shape=like((kinds, 2 * tokens, HEAD), BF16),
        compiler_params=params(),
        cost_estimate=cost(4 * tokens * width * columns, 4 * (tokens * width + width * columns)),
        name="project",
    )(near, far, *weights, bias)


def up_kernel(blocks, place_ref, near, far, *refs):
    weights, bias_ref, act_ref, slope_ref = refs[:blocks], *refs[blocks:]
    half = near.shape[0]
    depth = near.shape[1] // blocks
    for index, source in enumerate((near, far)):
        pre = bias_ref[...].astype(F32)
        for block, weight in enumerate(weights):
            pre = pre + dot(source[:, block * depth : (block + 1) * depth], weight[...], 1, 0)
        square = pre * pre
        wave = jnp.tanh(pre * (0.7978845608028654 + 0.7978845608028654 * 0.044715 * square))
        half_up = 0.5 + 0.5 * wave
        slope = half_up + (0.5 * pre) * (1.0 - wave * wave) * (
            0.7978845608028654 + 3.0 * 0.7978845608028654 * 0.044715 * square
        )
        rows = slice(index * half, (index + 1) * half)
        act_ref[rows, :] = (pre * half_up).astype(BF16)
        slope_ref[rows, :] = slope.astype(slope_ref.dtype)


def up_project(place, near, far, weight, bias):
    half, width = near.shape
    columns = weight.shape[1]
    tile = 512
    out_spec = pl.BlockSpec((2 * half, tile), lambda i, p: (0, i))
    return grid_call(
        functools.partial(up_kernel, weight.blocks),
        "up_project",
        place,
        (columns // tile,),
        [fixed((half, width))] * 2
        + weight.specs(1, tile)
        + [pl.BlockSpec((1, tile), lambda i, p: (0, i))],
        [out_spec] * 2,
        [like((2 * half, columns), BF16)] * 2,
        [],
        cost(4 * half * width * columns, 2 * width * (2 * half + columns) + 8 * half * columns),
        [near, far, *weight.arrays(), bias],
    )


def act_back_kernel(blocks, place_ref, near, far, *refs):
    weights, slope_ref, out_ref, sum_ref = refs[:blocks], *refs[blocks:]
    half = near.shape[0]
    depth = near.shape[1] // blocks
    total = None
    for index, source in enumerate((near, far)):
        grad = None
        for block, weight in enumerate(weights):
            part = dot(source[:, block * depth : (block + 1) * depth], weight[...], 1, 1)
            grad = part if grad is None else grad + part
        rows = slice(index * half, (index + 1) * half)
        low = (grad * slope_ref[rows, :].astype(F32)).astype(BF16)
        out_ref[rows, :] = low
        part = jnp.sum(low.astype(F32), axis=0, keepdims=True)
        total = part if total is None else total + part
    sum_ref[...] = total


def act_back(place, near, far, weight, slope):
    half, width = near.shape
    columns = weight.shape[0]
    tile = 512
    out_spec = pl.BlockSpec((2 * half, tile), lambda i, p: (0, i))
    return grid_call(
        functools.partial(act_back_kernel, weight.blocks),
        "act_back",
        place,
        (columns // tile,),
        [fixed((half, width))] * 2 + weight.specs(0, tile) + [out_spec],
        [out_spec, pl.BlockSpec((1, tile), lambda i, p: (0, i))],
        [like((2 * half, columns), BF16), like((1, columns), F32)],
        [],
        cost(4 * half * width * columns, 2 * width * (2 * half + columns) + 8 * half * columns),
        [near, far, *weight.arrays(), slope],
    )


def head_back_kernel(blocks, place_ref, near, far, *refs):
    weights, out = refs[:blocks], refs[blocks]
    half = near.shape[0]
    depth = near.shape[1] // blocks
    for index, source in enumerate((near, far)):
        grad = None
        for block, weight in enumerate(weights):
            part = dot(source[:, block * depth : (block + 1) * depth], weight[...], 1, 1)
            grad = part if grad is None else grad + part
        low = grad.astype(BF16)
        for slot in range(out.shape[0]):
            out[slot, index * half : (index + 1) * half, :] = low[:, slot * HEAD : (slot + 1) * HEAD]


def head_back(place, near, far, weight):
    half, width = near.shape
    columns = weight.shape[0]
    heads = columns // HEAD
    return grid_call(
        functools.partial(head_back_kernel, weight.blocks),
        "head_back",
        place,
        (1,),
        [fixed((half, width))] * 2 + weight.specs(0, columns),
        fixed((heads, 2 * half, HEAD)),
        like((heads, 2 * half, HEAD), BF16),
        [],
        cost(4 * half * width * columns, 2 * width * (2 * half + columns)),
        [near, far, *weight.arrays()],
    )


def terms_kernel(transposed, blocks, parts, place_ref, left_ref, *refs):
    weights = refs[: blocks * parts]
    sent, kept, *rest = refs[blocks * parts :]
    at = pl.program_id(0)
    left = left_ref
    if rest:
        left = rest[0]

        @pl.when(at == 0)
        def _():
            if len(left_ref.shape) == 3:
                for head in range(left_ref.shape[0]):
                    left[:, head * HEAD : (head + 1) * HEAD] = left_ref[head]
            else:
                heads, kinds = left_ref.shape[:2]
                for head in range(heads):
                    for kind in range(kinds):
                        column = (kind * heads + head) * HEAD
                        left[:, column : column + HEAD] = left_ref[head, kind]
                rest[1][...] = jnp.sum(left[...].astype(F32), axis=0, keepdims=True)

    half = sent.shape[0]
    depth = left.shape[1] // parts
    share = sent.shape[1] // blocks
    for block in range(blocks):
        acc = None
        for part in range(parts):
            weight = weights[part * blocks + block]
            here = dot(
                left[:, part * depth : (part + 1) * depth], weight[...], 1, 1 if transposed else 0
            )
            acc = here if acc is None else acc + here
        tile = acc.shape[1]
        columns = pl.ds(pl.multiple_of(block * share + at * tile, tile), tile)
        kept[:, columns] = acc[:half]
        sent[:, columns] = acc[half:].astype(BF16)


def terms(place, left, weights, transposed, tile):
    tokens = left.shape[-2]
    blocks, parts = weights[0].blocks, len(weights)
    out_axis = 0 if transposed else 1
    share = weights[0].shape[out_axis]
    tile = min(tile, share)
    depth = math.prod(left.shape) // tokens
    half = tokens // 2
    outs = [like((half, blocks * share), BF16), like((half, blocks * share), F32)]
    if left.ndim > 2:
        outs.append(like((tokens, depth), BF16))
    if left.ndim > 3:
        outs.append(like((1, depth), F32))
    return grid_call(
        functools.partial(terms_kernel, transposed, blocks, parts),
        "terms",
        place,
        (share // tile,),
        [fixed(left.shape)] + [spec for w in weights for spec in w.specs(out_axis, tile)],
        [fixed(v.shape) for v in outs],
        outs,
        [],
        cost(
            2 * tokens * depth * blocks * share,
            2 * depth * (tokens + blocks * share) + 6 * half * blocks * share,
        ),
        [left] + [v for w in weights for v in w.arrays()],
    )


def grad_kernel(pairs, place_ref, *refs):
    out = refs[-1]
    acc = None
    for index in range(pairs):
        part = dot(refs[2 * index][...], refs[2 * index + 1][...], 0, 0)
        acc = part if acc is None else acc + part
    out[...] = acc.astype(out.dtype)


def weight_grad(pairs, rows, columns, place, blocks, split_left):
    row_from, row_count = rows
    col_from, col_count = columns
    row_tile = min(1024, row_count // blocks if split_left else row_count)
    col_tile = min(512, col_count if split_left else col_count // blocks)
    row_base, col_base = row_from // row_tile, col_from // col_tile
    specs, values, depth = [], [], 0
    row_per, col_per = row_count // blocks // row_tile, col_count // blocks // col_tile

    def turned(at, per, place_ref):
        return lax.rem(at // per + blocks - place_ref[0], blocks) * per + lax.rem(at, per)

    def left_map(first):
        if split_left:
            return lambda i, j, p: (first, turned(i, row_per, p))
        return lambda i, j, p: (first, i + row_base)

    def right_map(first):
        if split_left:
            return lambda i, j, p: (first, j + col_base)
        return lambda i, j, p: (first, turned(j, col_per, p))

    for (left, left_at), (right, right_at), height in pairs:
        specs.append(pl.BlockSpec((height, row_tile), left_map(left_at)))
        specs.append(pl.BlockSpec((height, col_tile), right_map(right_at)))
        values += [left, right]
        depth += height
    return pl.pallas_call(
        functools.partial(grad_kernel, len(pairs)),
        grid_spec=pltpu.PrefetchScalarGridSpec(
            num_scalar_prefetch=1,
            grid=(row_count // row_tile, col_count // col_tile),
            in_specs=specs,
            out_specs=pl.BlockSpec((row_tile, col_tile), lambda i, j, p: (i, j)),
        ),
        out_shape=like((row_count, col_count), BF16),
        compiler_params=params(),
        cost_estimate=cost(
            2 * row_count * col_count * depth,
            2 * (depth * row_count + depth * col_count + row_count * col_count),
        ),
        name="weight_grad",
    )(place, *values)


def joint_grad_kernel(rows, count, has_add, place_ref, *refs):
    heads, near, far = refs[:rows], refs[rows : rows + count], refs[rows + count : rows + 2 * count]
    out, scratch = refs[-2:]
    _, kinds, size, _ = heads[0].shape
    half = size // 2
    depth = rows * half

    @pl.when(pl.program_id(0) == 0)
    def _():
        for step in range(count):
            source = lax.rem(place_ref[0] + count - step, count)
            for row, head in enumerate(heads):
                for part in range(2):
                    start = ((step * 2 + part) * rows + row) * half
                    for kind in range(kinds):
                        scratch[start : start + half, kind * HEAD : (kind + 1) * HEAD] = head[
                            source, kind, part * half : (part + 1) * half, :
                        ]

    acc = None
    for index in range(2 * count):
        left = (near, far)[index % 2][index // 2]
        part = dot(left[...], scratch[index * depth : (index + 1) * depth, :], 0, 0)
        acc = part if acc is None else acc + part
    if has_add:
        acc = acc + refs[rows + 2 * count][...].astype(F32)
    out[...] = acc.astype(BF16)


def joint_grad_terms(place, near, far, heads, left_cols, add=None):
    row_from, rows = left_cols
    tile = min(256, rows)
    base = row_from // tile
    places, kinds, size, _ = heads[0].shape
    depth = near[0].shape[0]
    specs = [pl.BlockSpec(h.shape, lambda i, p: (0, 0, 0, 0)) for h in heads]
    specs += [pl.BlockSpec((depth, tile), lambda i, p: (0, i + base))] * (2 * places)
    values = [*heads, *near, *far]
    if add is not None:
        specs.append(pl.BlockSpec((tile, kinds * HEAD), lambda i, p: (i, 0)))
        values.append(add)
    return pl.pallas_call(
        functools.partial(joint_grad_kernel, len(heads), places, add is not None),
        grid_spec=pltpu.PrefetchScalarGridSpec(
            num_scalar_prefetch=1,
            grid=(rows // tile,),
            in_specs=specs,
            out_specs=pl.BlockSpec((tile, kinds * HEAD), lambda i, p: (i, 0)),
            scratch_shapes=[pltpu.VMEM((2 * places * depth, kinds * HEAD), BF16)],
        ),
        out_shape=like((rows, kinds * HEAD), BF16),
        compiler_params=params(),
        cost_estimate=cost(
            4 * places * depth * rows * kinds * HEAD, 4 * places * depth * (rows + kinds * HEAD)
        ),
        name="joint_grad",
    )(place, *values)


def gather_blocks(scratch, source):
    count, size, _ = source.shape
    for index in range(count):
        scratch[index * size : (index + 1) * size, :] = source[index]


def gather_kinds(place_ref, sources, scratches, turned=None):
    count = len(sources)
    for step, source in enumerate(sources):
        size = source.shape[1]
        start = lax.rem(place_ref[0] + count - step, count) * size
        rows = pl.ds(pl.multiple_of(start, size), size)
        for kind, scratch in enumerate(scratches):
            scratch[rows, :] = source[kind]
        if turned is not None:
            turned[:, rows] = source[1].T


def put_rows(out, at, query_block, value, lead=()):
    size = out.shape[-2]
    per = query_block // size
    for slot in range(per):
        out[(at * per + slot, *lead)] = value[slot * size : (slot + 1) * size]


def attend_kernel(parts, query_block, key_block, live, place_ref, *refs):
    seg_row, seg_col, out, mixed_ref, total_ref = refs[parts : parts + 5]
    qs, ks, vs, scores, top, total, mixed = refs[parts + 5 :]
    at = pl.program_id(0)
    count = qs.shape[0] // key_block

    @pl.when(at == 0)
    def _():
        gather_kinds(place_ref, refs[:parts], (qs, ks, vs))

    here = pl.ds(pl.multiple_of(at * query_block, query_block), query_block)
    query = qs[here, :]
    seg_query = seg_row[:, here]
    top[...] = jnp.full_like(top, NEGATIVE)
    total[...] = jnp.zeros_like(total)
    mixed[...] = jnp.zeros_like(mixed)

    def score(step, masked):
        rows = pl.ds(pl.multiple_of(step * key_block, key_block), key_block)
        raw = dot(ks[rows, :], query, 1, 1) * (LOG2E * SCALE)
        if masked:
            raw = jnp.where(seg_col[rows, 0:1] == seg_query, raw, NEGATIVE)
        scores[rows, :] = raw
        top[...] = jnp.maximum(top[...], jnp.max(raw, axis=0, keepdims=True))

    def first(step, carry):
        pl.when(live[at, step] == 1)(functools.partial(score, step, True))
        pl.when(live[at, step] == 2)(functools.partial(score, step, False))
        return carry

    def second(step, carry):
        @pl.when(live[at, step] > 0)
        def _():
            rows = pl.ds(pl.multiple_of(step * key_block, key_block), key_block)
            weight = jnp.exp2(scores[rows, :] - top[...])
            total[...] += jnp.sum(weight, axis=0, keepdims=True)
            mixed[...] += dot(vs[rows, :], weight.astype(BF16), 0, 0)

        return carry

    lax.fori_loop(0, count, first, 0)
    lax.fori_loop(0, count, second, 0)
    result = mixed[...] / total[...]
    mixed_ref[:, here] = result
    total_ref[:, here] = top[...] + jnp.log2(total[...])
    put_rows(out, at, query_block, result.T.astype(BF16))


def attend(row, place, heads, seg_row, seg_col, live):
    parts = len(heads)
    length = seg_row.shape[2]
    size = length // parts
    query_block, key_block = length // live.shape[1], length // live.shape[2]
    part_spec = pl.BlockSpec((3, size, HEAD), lambda i, s, p: (0, row, 0))
    whole = lambda i, s, p: (0, 0)
    return pl.pallas_call(
        functools.partial(attend_kernel, parts, query_block, key_block),
        grid_spec=pltpu.PrefetchScalarGridSpec(
            num_scalar_prefetch=2,
            grid=(length // query_block,),
            in_specs=[part_spec] * parts
            + [
                pl.BlockSpec((None, 1, length), lambda i, s, p: (row, 0, 0)),
                pl.BlockSpec((None, length, HEAD), lambda i, s, p: (row, 0, 0)),
            ],
            out_specs=[
                pl.BlockSpec((parts, size, HEAD), lambda i, s, p: (0, 0, 0)),
                pl.BlockSpec((HEAD, length), whole),
                pl.BlockSpec((1, length), whole),
            ],
            scratch_shapes=[pltpu.VMEM((length, HEAD), BF16)] * 3
            + [
                pltpu.VMEM((length, query_block), F32),
                pltpu.VMEM((1, query_block), F32),
                pltpu.VMEM((1, query_block), F32),
                pltpu.VMEM((HEAD, query_block), F32),
            ],
        ),
        out_shape=[
            like((parts, size, HEAD), BF16),
            like((HEAD, length), F32),
            like((1, length), F32),
        ],
        compiler_params=params(),
        cost_estimate=cost(4 * length * length * HEAD, 8 * length * HEAD, length * length // 2),
        name="attend",
    )(live[row], place, *heads, seg_row, seg_col)


def attend_back_kernel(parts, query_block, key_block, live, place_ref, *refs):
    g_in, seg_row, seg_col, mixed_ref, total_ref, out = refs[parts : parts + 6]
    qs, ks, vs, gs, kt, d_keys, d_values, d_query = refs[parts + 6 :]
    at = pl.program_id(0)
    count = qs.shape[0] // key_block

    @pl.when(at == 0)
    def _():
        gather_kinds(place_ref, refs[:parts], (qs, ks, vs), kt)
        gather_blocks(gs, g_in)
        d_keys[...] = jnp.zeros_like(d_keys)
        d_values[...] = jnp.zeros_like(d_values)

    here = pl.ds(pl.multiple_of(at * query_block, query_block), query_block)
    query = qs[here, :]
    grad = gs[here, :]
    seg_query = seg_row[:, here]
    log_total = total_ref[:, here]
    weighted = jnp.sum(mixed_ref[:, here] * grad.astype(F32).T, axis=0, keepdims=True)
    d_query[...] = jnp.zeros_like(d_query)

    def back(step, masked):
        rows = pl.ds(pl.multiple_of(step * key_block, key_block), key_block)
        key, value = ks[rows, :], vs[rows, :]
        raw = dot(key, query, 1, 1) * (LOG2E * SCALE)
        if masked:
            raw = jnp.where(seg_col[rows, 0:1] == seg_query, raw, NEGATIVE)
        probs = jnp.exp2(raw - log_total)
        d_scores = (probs * (dot(value, grad, 1, 1) - weighted)).astype(BF16)
        d_values[rows, :] += dot(probs.astype(BF16), grad, 1, 0)
        d_keys[rows, :] += dot(d_scores, query, 1, 0)
        d_query[...] += dot(kt[:, rows], d_scores, 1, 0)

    def step_of(step, carry):
        pl.when(live[at, step] == 1)(functools.partial(back, step, True))
        pl.when(live[at, step] == 2)(functools.partial(back, step, False))
        return carry

    lax.fori_loop(0, count, step_of, 0)
    put_rows(out, at, query_block, (d_query[...] * SCALE).T.astype(BF16), (0,))

    @pl.when(at == pl.num_programs(0) - 1)
    def _():
        size = out.shape[2]
        for slot in range(out.shape[0]):
            rows = slice(slot * size, (slot + 1) * size)
            out[slot, 1] = (d_keys[rows, :] * SCALE).astype(BF16)
            out[slot, 2] = d_values[rows, :].astype(BF16)


def attend_back(row, place, heads, grads, seg_row, seg_col, live, mixed, totals):
    parts = len(heads)
    length = seg_row.shape[2]
    size = length // parts
    query_block, key_block = length // live.shape[1], length // live.shape[2]
    part_spec = pl.BlockSpec((3, size, HEAD), lambda i, s, p: (0, row, 0))
    whole = lambda i, s, p: (0, 0)
    return pl.pallas_call(
        functools.partial(attend_back_kernel, parts, query_block, key_block),
        grid_spec=pltpu.PrefetchScalarGridSpec(
            num_scalar_prefetch=2,
            grid=(length // query_block,),
            in_specs=[part_spec] * parts
            + [
                pl.BlockSpec((parts, size, HEAD), lambda i, s, p: (0, 0, 0)),
                pl.BlockSpec((None, 1, length), lambda i, s, p: (row, 0, 0)),
                pl.BlockSpec((None, length, HEAD), lambda i, s, p: (row, 0, 0)),
                pl.BlockSpec((HEAD, length), whole),
                pl.BlockSpec((1, length), whole),
            ],
            out_specs=pl.BlockSpec((parts, 3, size, HEAD), lambda i, s, p: (0, 0, 0, 0)),
            scratch_shapes=[pltpu.VMEM((length, HEAD), BF16)] * 4
            + [pltpu.VMEM((HEAD, length), BF16)]
            + [pltpu.VMEM((length, HEAD), F32)] * 2
            + [pltpu.VMEM((HEAD, query_block), F32)],
        ),
        out_shape=like((parts, 3, size, HEAD), BF16),
        compiler_params=params(),
        cost_estimate=cost(10 * length * length * HEAD, 16 * length * HEAD, length * length // 2),
        name="attend_back",
    )(live[row], place, *heads, grads, seg_row, seg_col, mixed, totals)


def normalize(hidden):
    center = hidden - jnp.mean(hidden, axis=-1, keepdims=True)
    inverse = lax.rsqrt(jnp.mean(center * center, axis=-1, keepdims=True) + EPSILON)
    return center * inverse, inverse


def normalize_back(grad, normal, inverse):
    return inverse * (
        grad
        - jnp.mean(grad, axis=-1, keepdims=True)
        - normal * jnp.mean(grad * normal, axis=-1, keepdims=True)
    )


def add_up(ref, values):
    @pl.when(pl.program_id(0) == 0)
    def _():
        ref[...] = jnp.zeros_like(ref)

    ref[...] += jnp.concatenate([jnp.sum(v, axis=0, keepdims=True) for v in values], axis=0)


def norm_one_kernel(near, far, x, vectors, normal_ref, inverse_ref, low_ref):
    hidden = x[...].astype(F32) + (near[...].astype(F32) + far[...].astype(F32)) + vectors[0:1, :]
    normal, inverse = normalize(hidden)
    normal_ref[...] = normal
    inverse_ref[...] = jnp.broadcast_to(inverse, inverse_ref.shape)
    low_ref[...] = (normal * vectors[1:2, :] + vectors[2:3, :]).astype(BF16)


def norm_two_kernel(near, far, normal_one, grad_ref, vectors, out_ref, second_ref, low_ref, sum_ref):
    hidden = (
        normal_one[...] * vectors[1:2, :]
        + vectors[2:3, :]
        + (near[...].astype(F32) + far[...].astype(F32))
        + vectors[3:4, :]
    )
    normal, inverse = normalize(hidden)
    out_ref[...] = (normal * vectors[4:5, :] + vectors[5:6, :]).astype(BF16)
    grad = grad_ref[...].astype(F32)
    d_hidden = normalize_back(grad * vectors[4:5, :], normal, inverse)
    low = d_hidden.astype(BF16)
    second_ref[...] = d_hidden
    low_ref[...] = low
    add_up(sum_ref, (low.astype(F32), grad * normal, grad))


def norm_back_kernel(near, far, second, normal_ref, inverse_ref, vectors, first_ref, low_ref, sum_ref):
    d_norm = second[...] + (near[...].astype(F32) + far[...].astype(F32))
    normal = normal_ref[...]
    d_hidden = normalize_back(d_norm * vectors[1:2, :], normal, inverse_ref[:, 0:1])
    low = d_hidden.astype(BF16)
    first_ref[...] = d_hidden
    low_ref[...] = low
    add_up(sum_ref, (low.astype(F32), d_norm * normal, d_norm))


def by_tokens(kernel, name, inputs, vectors, outs, sums=0):
    tokens, width = inputs[0][0].shape
    tile = tokens // 2
    specs = [
        pl.BlockSpec((tile, v.shape[1]), lambda i, a=at: (a * 2 + i, 0)) for v, at in inputs
    ]
    out_specs = [pl.BlockSpec((tile, columns), lambda i: (i, 0)) for columns, _ in outs]
    out_shape = [like((tokens, columns), dtype) for columns, dtype in outs]
    if sums:
        out_specs.append(pl.BlockSpec((sums, width), lambda i: (0, 0)))
        out_shape.append(like((sums, width), F32))
    return pl.pallas_call(
        kernel,
        grid=(2,),
        in_specs=specs + [pl.BlockSpec(vectors.shape, lambda i: (0, 0))],
        out_specs=out_specs,
        out_shape=out_shape,
        compiler_params=params(),
        cost_estimate=cost(20 * tokens * width, 16 * tokens * width),
        name=name,
    )(*[v for v, _ in inputs], vectors)


def local(
    layer_input,
    segment_ids,
    qkv_weight,
    qv_bias,
    out_weight,
    out_bias,
    norm1_gain,
    norm1_bias,
    up_weight,
    up_bias,
    down_weight,
    down_bias,
    norm2_gain,
    norm2_bias,
    out_grad,
):
    rows, local_len, width = layer_input.shape
    fsdp, ctx = lax.axis_size("fsdp"), lax.axis_size("ctx")
    y, place = lax.axis_index("fsdp"), lax.axis_index("ctx")
    core, chip = lax.axis_index("tp") % 2, lax.axis_index("tp") // 2
    columns = qkv_weight.shape[2]
    hidden_units = up_weight.shape[1]
    heads = columns // HEAD
    half = local_len // 2
    share = width // fsdp
    each = range(rows)
    assert heads == ctx == 4 and lax.axis_size("tp") == 4
    order = Order()

    def features(value):
        return rotate(value, value.ndim - 1, y, fsdp)

    def features_back(value):
        return rotate(value, value.ndim - 1, (fsdp - y) % fsdp, fsdp)

    def spread(block):
        return [block] + [shift(block, "fsdp", -by) for by in range(1, fsdp)]

    def swap_ctx(value):
        return lax.all_to_all(value, "ctx", 0, 0, tiled=True)

    def from_all(value):
        return swap_ctx(jnp.broadcast_to(value[None], (ctx, *value.shape)))

    def both(value):
        return value, core_swap(value)

    seg_own = rotate(segment_ids, 1, core, 2)
    seg = from_all(seg_own).transpose(1, 0, 2).reshape(rows, ctx * local_len)

    first_token = core * half + chip * (half // 2)
    quarter = features(lax.dynamic_slice_in_dim(layer_input, first_token, half // 2, axis=1))
    x_rows = features(rotate(layer_input, 1, core, 2))
    x = x_rows.reshape(rows * local_len, width)

    vectors = features(
        jnp.stack([out_bias, norm1_gain, norm1_bias, down_bias, norm2_gain, norm2_bias])
    ).astype(F32)
    grad_half = features(
        lax.dynamic_slice_in_dim(out_grad, core * half, half, axis=1)
    ).reshape(rows * half, width)

    fsdp_place = y.astype(jnp.int32)[None]
    ctx_place = place.astype(jnp.int32)[None]

    mine = lax.dynamic_slice_in_dim(qkv_weight, place * HEAD, HEAD, axis=2)
    head_weight = spread(mine.reshape(share, 3 * HEAD))
    bias_pair = lax.dynamic_slice_in_dim(qv_bias, place * HEAD, HEAD, axis=1)
    head_bias = jnp.concatenate(
        [bias_pair[:1], jnp.zeros_like(bias_pair[:1]), bias_pair[1:]], axis=1
    )

    def joined(quarter, other):
        parts = jnp.stack([quarter, other], axis=1).reshape(rows, half, width)
        return rotate(parts, 1, chip, 2).reshape(rows * half, width)

    def flat(value):
        return value.reshape(rows * half, width)

    x_near, x_far = [flat(x_rows[:, :half])], [flat(x_rows[:, half:])]
    first_quarter = shift(quarter, "ctx", 1)
    first_quarter, seg = lax.optimization_barrier((first_quarter, seg))
    heads_all = [project(x_near[0], x_far[0], rows, head_weight, head_bias)]
    second_quarter = shift(first_quarter, "ctx", 1)
    x_near.append(joined(first_quarter, chip_swap(first_quarter)))
    x_far.append(core_swap(x_near[1]))
    third_quarter = shift(after(second_quarter, x_near[1]), "ctx", 1)
    heads_all.append(project(x_near[1], x_far[1], rows, head_weight, head_bias))
    x_near.append(joined(second_quarter, chip_swap(second_quarter)))
    x_far.append(core_swap(x_near[2]))
    heads_all.append(project(x_near[2], x_far[2], rows, head_weight, head_bias))
    third_other = chip_swap(after(third_quarter, heads_all[0]))
    third_quarter = after(third_quarter, heads_all[1], heads_all[2])
    x_near.append(joined(third_quarter, third_other))
    x_far.append(core_swap(x_near[3]))
    heads_all.append(order.done(project(x_near[3], x_far[3], rows, head_weight, head_bias)))

    gate = [*head_weight[1:], first_quarter]

    def whole(block, axis):
        return lax.all_gather(after(block, *gate), "fsdp", axis=axis, tiled=True)

    out_full = Weight([whole(out_weight, 1)], 1, fsdp)
    up_full = Weight([whole(up_weight, 0)], 0, fsdp)
    down_full = Weight([whole(down_weight, 1)], 1, fsdp)
    joint_full = whole(jnp.stack([qkv_weight[:, j] for j in range(3)]), 1)
    joint_matrices = [Weight([joint_full], 0, fsdp, j) for j in range(3)]

    length = ctx * local_len
    seg_row = seg[:, None, :]
    seg_col = jnp.broadcast_to(seg[:, :, None], (rows, length, HEAD))

    def span(size):
        blocks = seg.reshape(rows, length // size, size)
        return jnp.min(blocks, axis=2), jnp.max(blocks, axis=2)

    (query_low, query_high), (key_low, key_high) = span(2 * local_len), span(local_len)
    meets = (query_low[:, :, None] <= key_high[:, None, :]) & (
        key_low[:, None, :] <= query_high[:, :, None]
    )
    same = (query_low == query_high)[:, :, None] & (key_low == key_high)[:, None, :] & meets
    live = meets.astype(jnp.int32) + same.astype(jnp.int32)

    attended, kept = [], []
    for r in each:
        pieces, mixed, totals = attend(
            r, ctx_place, [order.ready(heads_all[0]), *heads_all[1:]], seg_row, seg_col, live
        )
        order.done(totals)
        kept.append((mixed, totals))
        attended.append(swap_ctx(pieces))

    def begin(left, weights, transposed, tile):
        sent, mine, *rest = terms(order.ready(fsdp_place), left, weights, transposed, tile)
        order.done(sent)
        return core_swap(sent), mine, *rest

    def middle(near, mine):
        total = order.done((order.ready(mine) + near.astype(F32)).astype(BF16))
        return total, chip_swap(total)

    parts = [begin(attended[r], [out_full], False, 512) for r in each]
    attended_last = attended[-1]
    attended = [parts[r][2] for r in each]
    totals = [middle(*parts[r][:2]) for r in each]

    normal_one, inverse_one, norm_low = [], [], []
    act_low, slopes = [], []
    for r in each:
        near, far = totals[r]
        normal, inverse, low = by_tokens(
            norm_one_kernel,
            "norm_one",
            [(order.ready(near), 0), (far, 0), (x, 2 * r)],
            vectors,
            [(width, F32), (HEAD, F32), (width, BF16)],
        )
        order.done(low)
        normal_one.append(normal)
        inverse_one.append(inverse)
        norm_low.append(both(low))
        near, far = norm_low[r]
        act, slope = up_project(order.ready(fsdp_place), near, far, up_full, up_bias[None])
        order.done(act)
        act_low.append(act)
        slopes.append(slope)

    parts = [begin(act_low[r], [down_full], False, 512) for r in each]
    totals = [middle(*parts[r]) for r in each]

    layer_low, second, mlp_low, sums_two = [], [], [], []
    pre_low, up_sums, up_parts = [], [], []

    def norm_two(r):
        near, far = totals[r]
        out, d_second, low, sums = by_tokens(
            norm_two_kernel,
            "norm_two",
            [(order.ready(near), 0), (far, 0), (normal_one[r], 0), (grad_half, r)],
            vectors,
            [(width, BF16), (width, F32), (width, BF16)],
            3,
        )
        order.done(low)
        layer_low.append(out)
        second.append(d_second)
        mlp_low.append(both(low))
        sums_two.append(sums)

    def act_step(r):
        near, far = mlp_low[r]
        low, sums = act_back(fsdp_place, order.ready(near), far, down_full, slopes[r])
        order.done(low)
        pre_low.append(low)
        up_sums.append(sums)

    def up_step(r):
        up_parts.append(begin(pre_low[r], [up_full], True, 512))

    halves = range(2)
    gradients = {}

    def pairs_of(left, right):
        made = []
        for r in each:
            for h in halves:
                a = (left[r][h], 0) if isinstance(left[r], tuple) else (left[r], h)
                b = (right[r][h], 0) if isinstance(right[r], tuple) else (right[r], h)
                made.append((a, b, half))
        return made

    def give(name, pairs, shape, split_left, piece, pieces):
        (left, *others) = pairs
        left = ((order.ready(left[0][0]), left[0][1]), *left[1:])
        if split_left:
            part = shape[1] // pieces
            ranges = (0, shape[0]), (piece * part, part)
        else:
            part = shape[0] // pieces
            ranges = (piece * part, part), (0, shape[1])
        mine = order.done(
            weight_grad([left, *others], *ranges, fsdp_place, fsdp, split_left)
        )
        gradients[name, piece] = lax.psum_scatter(
            mine, "fsdp", scatter_dimension=0 if split_left else 1, tiled=True
        )

    def line_one(value):
        return value, lax.ppermute(value, "ctx", [(0, 1), (3, 2)])

    def line_two(value, other):
        pair = order.done((order.ready(value).astype(F32) + other.astype(F32)).astype(BF16))
        return pair, lax.ppermute(pair, "ctx", [(1, 2), (2, 1)])

    def line_three(pair, other):
        total = order.done((order.ready(pair).astype(F32) + other.astype(F32)).astype(BF16))
        return total, lax.ppermute(total, "ctx", [(1, 0), (2, 3)])

    outer = (place == 0) | (place == ctx - 1)

    def line_end(total, other):
        return jnp.where(outer, other, total)

    first, attn_low, sums_one, head_grads = [], [], [], []

    def norm_back(r):
        near, far = up_totals[r]
        d_first, low, sums = by_tokens(
            norm_back_kernel,
            "norm_back",
            [(order.ready(near), 0), (far, 0), (second[r], 0), (normal_one[r], 0), (inverse_one[r], 0)],
            vectors,
            [(width, F32), (width, BF16)],
            3,
        )
        order.done(low)
        first.append(d_first)
        attn_low.append(both(low))
        sums_one.append(sums)

    def head_step(r):
        near, far = attn_low[r]
        pieces = order.done(head_back(fsdp_place, order.ready(near), far, out_full))
        head_grads.append(swap_ctx(pieces))

    joint_back, joint_rows = [], []

    def attend_step(r):
        mixed, row_totals = kept[r]
        place_now = order.ready(ctx_place)
        pieces = attend_back(
            r, place_now, heads_all, head_grads[r], seg_row, seg_col, live, mixed, row_totals
        )
        joint_back.append(order.done(pieces))
        joint_rows.append(swap_ctx(pieces))

    lined = {}

    def line_start(name, piece):
        lined[name, piece] = line_one(gradients[name, piece])

    def line_step(step, name, piece):
        lined[name, piece] = step(*lined[name, piece])

    def small_start(value):
        value = value + shift(value, "fsdp", 1) if fsdp == 2 else lax.psum(value, "fsdp")
        return value, lax.ppermute(value, "ctx", [(0, 1), (1, 0), (2, 3), (3, 2)])

    def small_step(value, other):
        value = order.done(order.ready(value) + other)
        return value, lax.ppermute(value, "ctx", [(0, 2), (2, 0), (1, 3), (3, 1)])

    def small_end(value, other):
        return order.done(order.ready(value) + other)

    norm_two(0)
    act_step(0)
    up_step(0)
    order.pin(joint_full)
    norm_two(1)
    up_totals = [middle(*up_parts[0])]
    down_args = (pairs_of(act_low, mlp_low), (hidden_units, width), False)
    give("down", *down_args, 0, 2)
    act_step(1)
    up_step(1)
    give("down", *down_args, 1, 2)
    up_totals.append(middle(*up_parts[1]))
    up_args = (pairs_of(norm_low, pre_low), (width, hidden_units), True)
    norm_back(0)
    give("up", *up_args, 0, 2)
    order.pin(gradients["down", 0])
    head_step(0)
    line_start("down", 0)
    order.pin(head_grads[0])
    line_step(line_two, "down", 0)
    norm_back(1)
    order.pin(gradients["down", 1])
    give("up", *up_args, 1, 2)
    line_start("down", 1)
    head_step(1)
    out_args = (pairs_of(attended, attn_low), (columns, width), False)
    give("out", *out_args, 0, 1)
    wide = features_back(jnp.concatenate([sum(sums_two), sum(sums_one)], axis=0))
    wide = wide + core_swap(wide)
    attend_step(0)
    wide_small = small_start(jnp.concatenate([wide.reshape(-1), sum(up_sums).reshape(-1)]))
    order.pin(gradients["up", 0])
    line_step(line_three, "down", 0)
    line_step(line_two, "down", 1)
    line_start("up", 0)
    attend_step(1)

    arrived = None
    for by in range(1, fsdp):
        sent = joint_grad_terms(
            ctx_place, [order.ready(x_near[0])] + x_near[1:], x_far, joint_back, (by * share, share)
        )
        got = shift(order.done(sent), "fsdp", by)
        arrived = got if arrived is None else (arrived.astype(F32) + got.astype(F32))

    order.pin(gradients["up", 1])
    line_step(line_three, "down", 1)
    line_step(line_two, "up", 0)
    line_start("up", 1)
    wide_small = small_step(*wide_small)
    order.pin(arrived)
    in_parts = [begin(joint_rows[0], joint_matrices, True, 512)]
    mine = joint_grad_terms(
        ctx_place, [order.ready(x_near[0])] + x_near[1:], x_far, joint_back, (0, share), add=arrived
    )
    order.done(mine)
    in_totals = [middle(*in_parts[0][:2])]
    order.pin(gradients["out", 0])
    line_step(line_three, "up", 0)
    line_step(line_two, "up", 1)
    line_start("out", 0)
    wide_small = small_end(*wide_small)
    in_parts.append(begin(joint_rows[1], joint_matrices, True, 512))
    joint_all = from_all(mine)
    in_totals.append(middle(*in_parts[1][:2]))
    bias_sums = sum(p[3] for p in in_parts)
    late_small = small_start(
        jnp.concatenate([bias_sums[0, :columns], bias_sums[0, 2 * columns :]])
    )
    line_step(line_three, "up", 1)
    line_step(line_two, "out", 0)
    late_small = small_step(*late_small)
    line_step(line_three, "out", 0)
    late_small = small_end(*late_small)

    input_low = []
    for r in each:
        near, far = in_totals[r]
        input_low.append(both((first[r] + (near.astype(F32) + far.astype(F32))).astype(BF16)))

    def whole_rows(values):
        stacked = jnp.stack([jnp.concatenate(pair, axis=0) for pair in values])
        return features_back(rotate(stacked, 1, core, 2))

    layer_output = whole_rows([both(v) for v in layer_low])
    input_grad = whole_rows(input_low).astype(F32)

    joint_grad = (
        joint_all.reshape(ctx, share, 3, HEAD).transpose(1, 2, 0, 3).reshape(share, 3, columns)
    ).astype(F32)

    wide = wide_small[: 6 * width].reshape(6, width)
    up_bias_grad = wide_small[6 * width :]
    qv_bias_grad = late_small.reshape(2, columns)

    def final(name, pieces, axis=0):
        return jnp.concatenate(
            [line_end(*lined[name, p]) for p in range(pieces)], axis=axis
        ).astype(F32)

    return (
        layer_output,
        input_grad,
        joint_grad,
        qv_bias_grad,
        final("out", 1),
        wide[3],
        wide[4],
        wide[5],
        final("up", 2, 1),
        up_bias_grad,
        final("down", 2),
        wide[0],
        wide[1],
        wide[2],
    )


def solution(mesh):
    weights = P("fsdp", None, "tp"), P(None, "tp"), P("tp", "fsdp")
    tokens = P("fsdp", "ctx", None)
    up, down = P("fsdp", "tp"), P("tp", "fsdp")
    tail = (P(), P(), P(), up, P("tp"), down, P(), P(), P())
    return jax.shard_map(
        local,
        mesh=mesh,
        in_specs=(tokens, P("fsdp", "ctx"), *weights, *tail, tokens),
        out_specs=(tokens, tokens, *weights, *tail),
        check_vma=False,
    )
```
